256 devices in a mesh: fu: 8 (over x, core), fv: 16 (over z, y_hi), ch: 2 (over y_lo).
Axes of the slice: x: 4, y: 4 (y_hi: 2, y_lo: 2; y = y_hi * 2 + y_lo), z: 8, core: 2. Of those that a mesh axis runs over, the one named last changes fastest.
Arguments:
- u_cell: int32 [8, 6144], P('fu', 'fv'), may hold values from 0 to 504, as said below
- v_cell: int32 [8, 6144], P('fu', 'fv'), may hold values from 0 to 2040, as said below
- w_plane: int32 [8, 6144], P('fu', 'fv'), may hold values from 0 to 15
- counts: int32 [8, 48], P('fu', 'fv'), may hold values from 1 to 128, 3840 in all within a row
- vis_values: bfloat16 [128, 8, 6144], P('ch', 'fu', 'fv'), may hold values from -6 to 6
- kern_u: float32 [16, 8], replicated, may hold values from 0.2 to 1
- kern_v: float32 [16, 8], replicated, may hold values from 0.2 to 1
Outputs:
- grid: float32 [128, 512, 2048], P('ch', 'fu', 'fv')
The draws below stay inside these ranges and needn't reach their ends.
Inputs may be any that keep to these rules, and one draw needn't show every extreme that they name: Each row's u_cell lies in its own facet row's 64 cells, and the whole 8 by 8 support lies inside the grid. `v_cell`: the whole 8 by 8 support of each row lies inside the grid.
All inputs are finite; a program needn't handle non-finite values. No bound on the sum of `counts` on one device may be relied on, other than what follows from the above.
Results may differ from the reference program's by a relative error of at most 0.0039.
Values may be sent and summed in bfloat16 or wider, within the bound.
No kernel may reach another device: no remote copies, remote signals or barrier semaphores. Data moves between devices by JAX's collectives and lax.ppermute only.
A program may use at most 64 MiB of HBM per device.

```python
import math
import jax
import jax.numpy as jnp
import numpy as np
from jax import lax

CHG = 64
TAPS = 8
PLANES = 16
GU = 64
ROWS = 384
R = 128
NB = 3
NU = 512
NV = 2048
LIVE = 3840
N_FU = 8
N_FV = 16


def draw_u_cell(key, part):
    offsets = jax.random.randint(key, (N_FU, N_FV * ROWS), 0, GU)
    starts = jnp.arange(N_FU, dtype=jnp.int32)[:, None] * GU
    return jnp.minimum(starts + offsets, NU - 8).astype(jnp.int32)


def draw_v_cell(key, part):
    top = NV - 8
    half = top // 2
    first, second = jax.random.split(jax.random.fold_in(key, 7))
    left = jax.random.randint(first, (N_FU, N_FV * ROWS), 0, half + 1)
    right = jax.random.randint(second, (N_FU, N_FV * ROWS), 0, top - half + 1)
    result = (left + right).astype(jnp.int32)
    result = result.at[0, 0].set(0)
    result = result.at[N_FU - 1, N_FV * ROWS - 1].set(top)
    return result.astype(jnp.int32)


def place_ends(array, rng, least, largest):
    dims = array.shape
    index_at = [jax.random.randint(jax.random.fold_in(rng, axis), (), 0, dims[axis]) for axis in range(len(dims))]
    array = array.at[tuple(index_at)].set(least)
    longest = dims.index(max(dims))
    index_at[longest] = (index_at[longest] + 1) % dims[longest]
    return array.at[tuple(index_at)].set(largest)


def levels(stream_key, dims, cuts, smallest, top_value):
    def one(dim, blocks):
        heights = jax.random.uniform(jax.random.fold_in(jax.random.fold_in(stream_key, 6), dim), (blocks,), jnp.float32, smallest / len(cuts), top_value / len(cuts))
        return jnp.repeat(jnp.exp(heights), dims[dim] // blocks).reshape((-1,) + (1,) * (len(dims) - dim - 1))

    gain = one(*cuts[0])
    for cut in cuts[1:]:
        gain = gain * one(*cut)
    return gain


def length_profile(count, total, most, slope):
    loads = [(1 << 20) // math.isqrt(rank ** slope) + 1 for rank in range(2, count + 1)]
    rest, holding = total - most - (count - 1), [1] * (count - 1)
    while rest > 0:
        free = [i for i in range(count - 1) if holding[i] < most]
        whole, remaining = sum([loads[i] for i in free]), rest
        for i in free:
            extra = min(most - holding[i], max(1, remaining * loads[i] // whole), rest)
            holding[i] = holding[i] + extra
            rest = rest - extra
    return np.array([most] + holding)


def uneven(own_key, number_of, total, most, slope):
    if number_of == 2:
        one = jax.random.randint(own_key, (), max(1, total - most), min(most, total - 1) + 1)
        return jnp.stack([one, total - one])
    lengths = jnp.asarray(length_profile(number_of, total, most, slope), jnp.int32)
    pairs = (number_of - 1) // 2
    source_of, sink = lengths[1:1 + 2 * pairs:2], lengths[2:2 + 2 * pairs:2]
    margin = jnp.minimum(source_of - 1, most - sink)
    shifted = jax.random.randint(jax.random.fold_in(own_key, 1), (pairs,), 0, 1 << 20) % (margin + 1)
    lengths = lengths.at[1:1 + 2 * pairs:2].set(source_of - shifted).at[2:2 + 2 * pairs:2].set(sink + shifted)
    return lengths[jax.random.permutation(jax.random.fold_in(own_key, 2), number_of)]


def bell_draw(key, shape, scale, limit, shards=(), held_as=jnp.bfloat16):
    drawn = scale * jax.random.normal(key, shape, jnp.float32)
    if shards:
        drawn = drawn * levels(key, shape, shards, -0.22, 0.18)
    return jnp.clip(drawn, -limit, limit).astype(held_as)


def setup_inputs(seed: int = 0) -> dict:
    splits = jax.random.split(jax.random.key(seed), 8)
    u_cell = draw_u_cell(jax.random.fold_in(splits[7], 71), 0)
    v_cell = draw_v_cell(jax.random.fold_in(splits[7], 71), 0)
    w_plane = place_ends(jax.random.randint(splits[2], (N_FU, N_FV * ROWS), 0, PLANES), jax.random.fold_in(splits[2], 1), 0, PLANES - 1).astype(jnp.int32)
    counts = jax.vmap(lambda own: uneven(own, N_FV * NB, LIVE, R, 2))(jax.random.split(splits[3], N_FU)).reshape((N_FU, N_FV * NB)).astype(jnp.int32)
    vis_values = bell_draw(splits[4], (2 * CHG, N_FU, N_FV * ROWS), 1.0, 6.0, ((0, 2), (1, 8), (2, 16)))
    kern_u = jnp.clip(jax.random.uniform(splits[5], (PLANES, TAPS), jnp.float32, 0.2, 1.0), 0.2, 1.0)
    kern_v = jnp.clip(jax.random.uniform(splits[6], (PLANES, TAPS), jnp.float32, 0.2, 1.0), 0.2, 1.0)
    return {"u_cell": u_cell, "v_cell": v_cell, "w_plane": w_plane, "counts": counts, "vis_values": vis_values, "kern_u": kern_u, "kern_v": kern_v}


def reference(u_cell, v_cell, w_plane, counts, vis_values, kern_u, kern_v):
    taps = kern_u.shape[1]
    chans = vis_values.shape[0]
    position = jnp.arange(N_FV * ROWS, dtype=jnp.int32) % R
    live = (position[None, :] < jnp.repeat(counts, R, axis=1)).astype(jnp.int32)
    values = jnp.moveaxis(vis_values, 1, 0)
    bases = (jnp.arange(N_FU, dtype=jnp.int32) * GU).astype(jnp.int32)
    tap_ids = jnp.arange(taps, dtype=jnp.int32)

    def one_row(inputs):
        cu, cv, plane, alive, vals, base = inputs
        ku = kern_u[plane] * alive.astype(jnp.float32)[:, None]
        ku = ku.astype(jnp.bfloat16).astype(jnp.float32)
        kv = (vals.astype(jnp.float32)[:, :, None] * kern_v[plane][None]).astype(jnp.bfloat16).astype(jnp.float32)
        data = ku[None, :, :, None] * kv[:, :, None, :]
        row_ids = (cu - base)[:, None, None] + tap_ids[None, :, None]
        col_ids = cv[:, None, None] + tap_ids[None, None, :]
        seg_ids = (row_ids * NV + col_ids).astype(jnp.int32)
        summed = jax.ops.segment_sum(data.reshape(chans, -1).T, seg_ids.reshape(-1), num_segments=(GU + 8) * NV)
        return summed.T.reshape(chans, GU + 8, NV)

    stacked = lax.map(one_row, (u_cell, v_cell, w_plane, live, values, bases))
    main = stacked[:, :, :GU, :]
    over = stacked[:, :, GU:, :]
    main = main.at[1:, :, :8, :].add(over[:-1])
    return jnp.moveaxis(main, 0, 1).reshape(chans, NU, NV)
```

```python
import functools

import jax
import jax.numpy as jnp
from jax import lax
from jax.experimental import pallas as pl
from jax.experimental.pallas import tpu as pltpu
from jax.sharding import PartitionSpec as P

GU = 64
GV = 128
TAPS = 8
LANES = 128
META = 8
KT = 256
F32 = jnp.float32
BF16 = jnp.bfloat16
NT = (((1,), (1,)), ((), ()))


def pack_kernel(cap, n_dst, u_ref, v_ref, w_ref, counts_ref, vis_ref, out_ref):
    chans, _, rows = vis_ref.shape
    n_blocks = counts_ref.shape[1]
    block = rows // n_blocks
    u, v, w = u_ref[...], v_ref[...], w_ref[...]
    lane = lax.broadcasted_iota(jnp.int32, (1, rows), 1)
    limit = jnp.zeros((1, rows), jnp.int32)
    for b in range(n_blocks):
        limit = jnp.where(lane >= b * block, b * block + counts_ref[0, b], limit)
    live = lane < limit
    first = v // GV
    last = (v + (TAPS - 1)) // GV
    dst = lax.broadcasted_iota(jnp.int32, (n_dst, rows), 0)
    member = ((dst == first) | (dst == last)) & live
    member_f = member.astype(F32)
    before = lax.broadcasted_iota(jnp.int32, (rows, rows), 0) < lax.broadcasted_iota(
        jnp.int32, (rows, rows), 1
    )
    rank = jnp.dot(
        member_f.astype(BF16),
        before.astype(F32).astype(BF16),
        preferred_element_type=F32,
    )
    rank = jnp.where(member, rank.astype(jnp.int32), -1)
    total = jnp.sum(member_f, axis=1, keepdims=True)
    over = (jnp.max(total, axis=0, keepdims=True) > cap).astype(F32)
    meta = jnp.concatenate(
        [
            (u % GU).astype(F32),
            (v % GV).astype(F32),
            first.astype(F32),
            w.astype(F32),
            jnp.zeros((META - 4, rows), F32),
        ],
        axis=0,
    ).astype(BF16)
    vis = vis_ref[:, 0, :]
    slot = lax.broadcasted_iota(jnp.int32, (cap, rows), 0)
    row_id = lax.broadcasted_iota(jnp.int32, (META, cap), 0)
    for d in range(n_dst):
        pick = (slot == rank[d : d + 1, :]).astype(F32).astype(BF16)
        sent = lax.dot_general(vis, pick, NT, preferred_element_type=F32)
        tags = lax.dot_general(meta, pick, NT, preferred_element_type=F32)
        held = jnp.minimum(total[d : d + 1, :], float(cap))
        tags = jnp.where(row_id == 4, over, tags)
        tags = jnp.where(row_id == 5, jnp.floor(held / 64.0), tags)
        tags = jnp.where(row_id == 6, held - 64.0 * jnp.floor(held / 64.0), tags)
        out_ref[d, :chans, :] = sent.astype(BF16)
        out_ref[d, chans:, :] = tags.astype(BF16)


def pack(cap, n_dst, u, v, w, counts, vis):
    chans = vis.shape[0]
    vmem = pl.BlockSpec(memory_space=pltpu.VMEM)
    return pl.pallas_call(
        functools.partial(pack_kernel, cap, n_dst),
        out_shape=jax.ShapeDtypeStruct((n_dst, chans + META, cap), BF16),
        in_specs=[vmem, vmem, vmem, pl.BlockSpec(memory_space=pltpu.SMEM), vmem],
        out_specs=vmem,
        compiler_params=pltpu.CompilerParams(vmem_limit_bytes=48 << 20),
    )(u, v, w, counts, vis)


def tap_rows(table, plane):
    result = jnp.zeros((TAPS, plane.shape[1]), F32)
    for p in range(table.shape[1]):
        result = jnp.where(plane == p, table[:, p : p + 1], result)
    return result


def spread(taps, start, low, span):
    cell = lax.broadcasted_iota(jnp.int32, (span, taps.shape[1]), 0) + (low - start)
    result = jnp.zeros((span, taps.shape[1]), F32)
    for t in range(TAPS):
        result = jnp.where(cell == t, taps[t : t + 1, :], result)
    return result


def v_weights(tags, plane, kern_v, facet):
    start = tags[1:2, :] + GV * (tags[2:3, :] - facet)
    wide = spread(tap_rows(kern_v, plane), start, 0, GV)
    high = wide.astype(BF16)
    low = (wide - high.astype(F32)).astype(BF16)
    return jnp.concatenate([high, low], axis=0)


def weighted(vis, ku):
    chans, span, lanes = vis.shape[0], ku.shape[0], vis.shape[1]
    full = vis[:, None, :] * ku[None, :, :]
    return full.reshape(chans * span, lanes).astype(BF16)


def border_kernel(msgs_ref, kern_u_ref, kern_v_ref, held_ref, tiles_ref, halo_ref, acc):
    n_src, depth, cap = msgs_ref.shape
    chans = depth - META
    facet = lax.axis_index("fv")
    parts = cap // LANES
    last_tile = held_ref.shape[1] // LANES - 1
    lane = lax.broadcasted_iota(jnp.int32, (depth, LANES), 1)

    def put(tile, value):
        at = pl.multiple_of(tile * LANES, LANES)
        held_ref[:, pl.ds(at, LANES)] = value.astype(BF16)

    def add_source(src, state):
        offset, tile = state
        tags = msgs_ref[src, chans:, :LANES].astype(F32)
        length = (64.0 * jnp.max(tags[5:6, :]) + jnp.max(tags[6:7, :])).astype(jnp.int32)
        for part in range(parts):
            block = msgs_ref[src, :, part * LANES : (part + 1) * LANES].astype(F32)
            shift = offset % LANES
            turned = pltpu.roll(block, shift, 1)
            at = offset // LANES
            put(at, jnp.where(lane < shift, tile, turned))
            spill = jnp.where(lane < shift, turned, 0.0)
            put(at + 1, spill)
            here = jnp.clip(length - part * LANES, 0, LANES)
            crossed = shift + here >= LANES
            tile = jnp.where(crossed, spill, jnp.where(lane < shift, tile, turned))
            offset = offset + here
        return offset, tile

    offset, _ = lax.fori_loop(0, n_src, add_source, (0, jnp.zeros((depth, LANES), F32)))
    put(jnp.minimum(offset // LANES + 1, last_tile), jnp.zeros((depth, LANES), F32))
    tiles = (offset + KT - 1) // KT
    tiles_ref[0, 0] = tiles
    acc[...] = jnp.zeros_like(acc)
    kern_u, kern_v = kern_u_ref[...].T, kern_v_ref[...].T

    def step(k, _):
        cols = pl.ds(pl.multiple_of(k * KT, KT), KT)
        vis = held_ref[:chans, cols].astype(F32)
        tags = held_ref[chans:, cols].astype(F32).astype(jnp.int32)
        plane = tags[3:4, :]
        ku = spread(tap_rows(kern_u, plane), tags[0:1, :], GU, TAPS)
        left = weighted(vis, ku.astype(BF16).astype(F32))
        right = v_weights(tags, plane, kern_v, facet)
        acc[...] += lax.dot_general(left, right, NT, preferred_element_type=F32)
        return 0

    lax.fori_loop(0, tiles, step, 0)
    halo_ref[...] = (acc[:, :GV] + acc[:, GV:]).reshape(chans, TAPS, GV).astype(BF16)


def border(msgs, kern_u, kern_v, width):
    n_src, depth, cap = msgs.shape
    chans = depth - META
    vmem = pl.BlockSpec(memory_space=pltpu.VMEM)
    return pl.pallas_call(
        border_kernel,
        out_shape=(
            jax.ShapeDtypeStruct((depth, width), BF16),
            jax.ShapeDtypeStruct((1, 1), jnp.int32),
            jax.ShapeDtypeStruct((chans, TAPS, GV), BF16),
        ),
        in_specs=[vmem] * 3,
        out_specs=(vmem, pl.BlockSpec(memory_space=pltpu.SMEM), vmem),
        scratch_shapes=[pltpu.VMEM((chans * TAPS, 2 * GV), F32)],
        compiler_params=pltpu.CompilerParams(vmem_limit_bytes=48 << 20),
    )(msgs, kern_u, kern_v)


def main_kernel(step_chans, tiles_ref, held_ref, kern_u_ref, kern_v_ref, out_ref, ku_s, kv_s, acc):
    chans = held_ref.shape[0] - META
    facet = lax.axis_index("fv")
    i = pl.program_id(0)
    tiles = tiles_ref[0, 0]

    @pl.when(i == 0)
    def _():
        kern_u, kern_v = kern_u_ref[...].T, kern_v_ref[...].T

        def prepare(k, _):
            cols = pl.ds(pl.multiple_of(k * KT, KT), KT)
            tags = held_ref[chans:, cols].astype(F32).astype(jnp.int32)
            plane = tags[3:4, :]
            ku_s[:, cols] = spread(tap_rows(kern_u, plane), tags[0:1, :], 0, GU).astype(BF16)
            kv_s[:, cols] = v_weights(tags, plane, kern_v, facet)
            return 0

        lax.fori_loop(0, tiles, prepare, 0)

    acc[...] = jnp.zeros_like(acc)
    first = pl.multiple_of(i * step_chans, step_chans)

    def step(k, _):
        cols = pl.ds(pl.multiple_of(k * KT, KT), KT)
        vis = held_ref[pl.ds(first, step_chans), cols].astype(F32)
        left = weighted(vis, ku_s[:, cols].astype(F32))
        acc[...] += lax.dot_general(left, kv_s[:, cols], NT, preferred_element_type=F32)
        return 0

    lax.fori_loop(0, tiles, step, 0)
    out_ref[...] = (acc[:, :GV] + acc[:, GV:]).reshape(step_chans, GU, GV)


def main(tiles, held, kern_u, kern_v, step_chans=8):
    depth, width = held.shape
    chans = depth - META
    vmem = pl.BlockSpec(memory_space=pltpu.VMEM)
    return pl.pallas_call(
        functools.partial(main_kernel, step_chans),
        grid=(chans // step_chans,),
        out_shape=jax.ShapeDtypeStruct((chans, GU, GV), F32),
        in_specs=[pl.BlockSpec(memory_space=pltpu.SMEM)] + [vmem] * 3,
        out_specs=pl.BlockSpec((step_chans, GU, GV), lambda i: (i, 0, 0)),
        scratch_shapes=[
            pltpu.VMEM((GU, width), BF16),
            pltpu.VMEM((2 * GV, width), BF16),
            pltpu.VMEM((step_chans * GU, 2 * GV), F32),
        ],
        compiler_params=pltpu.CompilerParams(
            dimension_semantics=("arbitrary",), vmem_limit_bytes=48 << 20
        ),
    )(tiles, held, kern_u, kern_v)


def join_kernel(grid_ref, halo_ref, out_ref):
    out_ref[...] = grid_ref[...] + halo_ref[...].astype(F32)


def join(grid, halo):
    chans = grid.shape[0]
    strip = pl.BlockSpec((chans, TAPS, GV), lambda i: (0, 0, 0))
    return pl.pallas_call(
        join_kernel,
        grid=(1,),
        out_shape=jax.ShapeDtypeStruct(grid.shape, grid.dtype),
        in_specs=[strip, strip],
        out_specs=strip,
        input_output_aliases={0: 0},
    )(grid, halo)


def per_device(u_cell, v_cell, w_plane, counts, vis_values, kern_u, kern_v):
    n_fv = lax.axis_size("fv")
    n_fu = lax.axis_size("fu")
    rows = u_cell.shape[1]
    chans = vis_values.shape[0]
    width = 4096
    small = 128

    def exchange(cap):
        sent = pack(cap, n_fv, u_cell, v_cell, w_plane, counts, vis_values)
        return lax.all_to_all(sent, "fv", 0, 0)

    msgs = exchange(small)
    over = jnp.max(msgs[:, chans + 4, 0]) > 0

    def whole():
        return border(exchange(rows), kern_u, kern_v, width)

    held, tiles, halo = lax.cond(over, whole, lambda: border(msgs, kern_u, kern_v, width))
    came = lax.ppermute(halo, "fu", [(i, i + 1) for i in range(n_fu - 1)])
    return join(main(tiles, held, kern_u, kern_v), came)


def solution(mesh):
    return jax.shard_map(
        per_device,
        mesh=mesh,
        in_specs=(
            P("fu", "fv"),
            P("fu", "fv"),
            P("fu", "fv"),
            P("fu", "fv"),
            P("ch", "fu", "fv"),
            P(),
            P(),
        ),
        out_specs=P("ch", "fu", "fv"),
        check_vma=False,
    )
```

```python
import functools

import jax
import jax.numpy as jnp
from jax import lax
from jax.experimental import pallas as pl
from jax.experimental.pallas import tpu as pltpu
from jax.sharding import PartitionSpec as P

GU = 64
GV = 128
TAPS = 8
LANES = 128
META = 8
KT = 256
F32 = jnp.float32
BF16 = jnp.bfloat16
NT = (((1,), (1,)), ((), ()))


def meta_rows(cap):
    return META * ((cap + LANES - 1) // LANES)


def pack_kernel(cap, n_dst, u_ref, v_ref, w_ref, counts_ref, vis_ref, out_ref):
    chans, rows = vis_ref.shape
    n_blocks = counts_ref.shape[1]
    block = rows // n_blocks
    half = cap // 2
    u, v, w = u_ref[...], v_ref[...], w_ref[...]
    lane = lax.broadcasted_iota(jnp.int32, (1, rows), 1)
    limit = jnp.zeros((1, rows), jnp.int32)
    for b in range(n_blocks):
        limit = jnp.where(lane >= b * block, b * block + counts_ref[0, b], limit)
    live = lane < limit
    first = v // GV
    last = (v + (TAPS - 1)) // GV
    dst = lax.broadcasted_iota(jnp.int32, (n_dst, rows), 0)
    member = ((dst == first) | (dst == last)) & live
    member_f = member.astype(F32)
    before = lax.broadcasted_iota(jnp.int32, (rows, rows), 0) < lax.broadcasted_iota(
        jnp.int32, (rows, rows), 1
    )
    rank = jnp.dot(
        member_f.astype(BF16),
        before.astype(F32).astype(BF16),
        preferred_element_type=F32,
    )
    rank = jnp.where(member, rank.astype(jnp.int32), -1)
    total = jnp.sum(member_f, axis=1, keepdims=True)
    over = (jnp.max(total, axis=0, keepdims=True) > cap).astype(F32)
    meta = jnp.concatenate(
        [
            (u % GU).astype(F32),
            (v % GV).astype(F32),
            first.astype(F32),
            w.astype(F32),
            jnp.zeros((META - 4, rows), F32),
        ],
        axis=0,
    ).astype(BF16)
    vis = vis_ref[...]
    blank = jnp.zeros_like(vis)
    low_lanes = jnp.concatenate([vis, blank], axis=0)
    high_lanes = jnp.concatenate([blank, vis], axis=0)
    slot = lax.broadcasted_iota(jnp.int32, (cap, rows), 0)
    row_id = lax.broadcasted_iota(jnp.int32, (META, 1), 0)
    for d in range(n_dst):
        pick = (slot == rank[d : d + 1, :]).astype(F32).astype(BF16)
        sent = lax.dot_general(pick[:half], low_lanes, NT, preferred_element_type=F32)
        sent += lax.dot_general(pick[half:], high_lanes, NT, preferred_element_type=F32)
        out_ref[d, :half, :] = sent.astype(BF16)
        held = jnp.minimum(total[d : d + 1, :], float(cap))
        coarse = jnp.floor(held / 64.0)
        tail = jnp.where(row_id == 4, over, 0.0)
        tail = jnp.where(row_id == 5, coarse, tail)
        tail = jnp.where(row_id == 6, held - 64.0 * coarse, tail)
        for p in range(0, cap, LANES):
            wide = min(LANES, cap - p)
            tags = lax.dot_general(meta, pick[p : p + wide], NT, preferred_element_type=F32)
            at = half + META * (p // LANES)
            if wide < LANES:
                tags = jnp.concatenate([tags, jnp.zeros((META, LANES - wide), F32)], axis=1)
            out_ref[d, at : at + META, :] = (tags + tail).astype(BF16)


def pack(cap, n_dst, u, v, w, counts, vis):
    vmem = pl.BlockSpec(memory_space=pltpu.VMEM)
    return pl.pallas_call(
        functools.partial(pack_kernel, cap, n_dst),
        out_shape=jax.ShapeDtypeStruct((n_dst, cap // 2 + meta_rows(cap), LANES), BF16),
        in_specs=[vmem, vmem, vmem, pl.BlockSpec(memory_space=pltpu.SMEM), vmem],
        out_specs=vmem,
        compiler_params=pltpu.CompilerParams(vmem_limit_bytes=10 << 20),
    )(u, v, w, counts, vis)


def tap_rows(table, plane):
    result = jnp.zeros((TAPS, plane.shape[1]), F32)
    for p in range(table.shape[1]):
        result = jnp.where(plane == p, table[:, p : p + 1], result)
    return result


def spread(taps, start, low, span):
    cell = lax.broadcasted_iota(jnp.int32, (span, taps.shape[1]), 0) + (low - start)
    result = jnp.zeros((span, taps.shape[1]), F32)
    for t in range(TAPS):
        result = jnp.where(cell == t, taps[t : t + 1, :], result)
    return result


def v_weights(tags, plane, kern_v, facet):
    start = tags[1:2, :] + GV * (tags[2:3, :] - facet)
    wide = spread(tap_rows(kern_v, plane), start, 0, GV)
    high = wide.astype(BF16)
    low = (wide - high.astype(F32)).astype(BF16)
    return jnp.concatenate([high, low], axis=0)


def weighted(vis, ku):
    chans, span, lanes = vis.shape[0], ku.shape[0], vis.shape[1]
    full = vis[:, None, :] * ku[None, :, :]
    return full.reshape(chans * span, lanes).astype(BF16)


def border_kernel(cap, chans, msgs_ref, kern_u_ref, kern_v_ref, held_ref, tiles_ref, halo_ref, rows_s, tags_s, acc):
    n_src = msgs_ref.shape[0]
    half = cap // 2
    facet = lax.axis_index("fv")
    lane = lax.broadcasted_iota(jnp.int32, (META, LANES), 1)

    def put(tile, value):
        tags_s[:, pl.ds(pl.multiple_of(tile * LANES, LANES), LANES)] = value

    lengths = []
    for src in range(n_src):
        tags = msgs_ref[src, half : half + META, :].astype(F32)
        lengths.append((64.0 * tags[5, 0] + tags[6, 0]).astype(jnp.int32))
    offset = 0
    tile = jnp.zeros((META, LANES), F32)
    for src in range(n_src):
        length = lengths[src]
        rows_s[pl.ds(offset, half), :] = msgs_ref[src, :half, :].astype(F32)

        @pl.when(length > half)
        def _(src=src, offset=offset):
            block = msgs_ref[src, :half, :].astype(F32)
            rows_s[pl.ds(offset + half, half), :] = pltpu.roll(block, LANES // 2, 1)

        for p in range(0, cap, LANES):
            at = half + META * (p // LANES)
            tags = msgs_ref[src, at : at + META, :].astype(F32)
            shift = offset % LANES
            turned = pltpu.roll(tags, shift, 1)
            where = offset // LANES
            tile = jnp.where(lane < shift, tile, turned)
            put(where, tile)
            spill = jnp.where(lane < shift, turned, 0.0)
            put(where + 1, spill)
            here = jnp.clip(length - p, 0, LANES)
            tile = jnp.where(shift + here >= LANES, spill, tile)
            offset = offset + here
    rows_s[pl.ds(offset, KT), :] = jnp.zeros((KT, LANES), F32)
    put(offset // LANES + 1, jnp.zeros((META, LANES), F32))
    tiles = jnp.maximum((offset + KT - 1) // KT, 1)
    tiles_ref[0, 0] = tiles
    acc[...] = jnp.zeros_like(acc)
    kern_u, kern_v = kern_u_ref[...], kern_v_ref[...]

    def step(k, _):
        at = pl.multiple_of(k * KT, KT)
        cols = pl.ds(at, KT)
        vis = rows_s[cols, :].T[:chans]
        tags = tags_s[:, cols]
        held_ref[:chans, cols] = vis.astype(BF16)
        held_ref[chans:, cols] = tags.astype(BF16)
        tags = tags.astype(jnp.int32)
        plane = tags[3:4, :]
        ku = spread(tap_rows(kern_u, plane), tags[0:1, :], GU, TAPS)
        left = weighted(vis, ku.astype(BF16).astype(F32))
        right = v_weights(tags, plane, kern_v, facet)
        acc[...] += lax.dot_general(left, right, NT, preferred_element_type=F32)
        return 0

    lax.fori_loop(0, tiles, step, 0)
    halo_ref[...] = (acc[:, :GV] + acc[:, GV:]).reshape(chans, TAPS, GV).astype(BF16)


def border(cap, chans, msgs, kern_u, kern_v, width):
    vmem = pl.BlockSpec(memory_space=pltpu.VMEM)
    return pl.pallas_call(
        functools.partial(border_kernel, cap, chans),
        out_shape=(
            jax.ShapeDtypeStruct((chans + META, width), BF16),
            jax.ShapeDtypeStruct((1, 1), jnp.int32),
            jax.ShapeDtypeStruct((chans, TAPS, GV), BF16),
        ),
        in_specs=[vmem] * 3,
        out_specs=(vmem, pl.BlockSpec(memory_space=pltpu.SMEM), vmem),
        scratch_shapes=[
            pltpu.VMEM((width + 2 * KT, LANES), F32),
            pltpu.VMEM((META, width + 2 * KT), F32),
            pltpu.VMEM((chans * TAPS, 2 * GV), F32),
        ],
        compiler_params=pltpu.CompilerParams(vmem_limit_bytes=12 << 20),
    )(msgs, kern_u, kern_v)


def main_kernel(step_chans, tiles_ref, held_ref, kern_u_ref, kern_v_ref, out_ref, strip_ref, ku_s, kv_s, acc):
    chans = held_ref.shape[0] - META
    facet = lax.axis_index("fv")
    i = pl.program_id(0)
    tiles = tiles_ref[0, 0]

    @pl.when(i == 0)
    def _():
        kern_u, kern_v = kern_u_ref[...], kern_v_ref[...]

        def prepare(k, _):
            cols = pl.ds(pl.multiple_of(k * KT, KT), KT)
            tags = held_ref[chans:, cols].astype(F32).astype(jnp.int32)
            plane = tags[3:4, :]
            ku_s[:, cols] = spread(tap_rows(kern_u, plane), tags[0:1, :], 0, GU).astype(BF16)
            start = tags[1:2, :] + GV * (tags[2:3, :] - facet)
            wide = spread(tap_rows(kern_v, plane), start, 0, GV).T
            high = wide.astype(BF16)
            kv_s[cols, :GV] = high
            kv_s[cols, GV:] = (wide - high.astype(F32)).astype(BF16)
            return 0

        lax.fori_loop(0, tiles, prepare, 0)

    first = pl.multiple_of(i * step_chans, step_chans)

    def emit(total):
        total = (total[:, :GV] + total[:, GV:]).reshape(step_chans, GU, GV)
        out_ref[...] = total
        strip_ref[pl.ds(first, step_chans)] = total[:, :TAPS, :]

    def product(cols):
        vis = held_ref[pl.ds(first, step_chans), cols].astype(F32)
        left = weighted(vis, ku_s[:, cols].astype(F32))
        return jnp.dot(left, kv_s[cols, :], preferred_element_type=F32)

    for n in (1, 2, 3):

        @pl.when(tiles == n)
        def _(n=n):
            emit(product(pl.ds(0, n * KT)))

    @pl.when(tiles > 3)
    def _():
        acc[...] = jnp.zeros_like(acc)

        def step(k, _):
            acc[...] += product(pl.ds(pl.multiple_of(k * KT, KT), KT))
            return 0

        lax.fori_loop(0, tiles, step, 0)
        emit(acc[...])


def main(tiles, held, kern_u, kern_v, step_chans=16):
    depth, width = held.shape
    chans = depth - META
    vmem = pl.BlockSpec(memory_space=pltpu.VMEM)
    return pl.pallas_call(
        functools.partial(main_kernel, step_chans),
        grid=(chans // step_chans,),
        out_shape=(
            jax.ShapeDtypeStruct((chans, GU, GV), F32),
            jax.ShapeDtypeStruct((chans, TAPS, GV), F32),
        ),
        in_specs=[pl.BlockSpec(memory_space=pltpu.SMEM)] + [vmem] * 3,
        out_specs=(
            pl.BlockSpec((step_chans, GU, GV), lambda i: (i, 0, 0)),
            vmem,
        ),
        scratch_shapes=[
            pltpu.VMEM((GU, width), BF16),
            pltpu.VMEM((width, 2 * GV), BF16),
            pltpu.VMEM((step_chans * GU, 2 * GV), F32),
        ],
        compiler_params=pltpu.CompilerParams(
            dimension_semantics=("arbitrary",), vmem_limit_bytes=16 << 20
        ),
    )(tiles, held, kern_u, kern_v)


def join_kernel(_, strip_ref, halo_ref, out_ref, total, sem):
    total[...] = strip_ref[...] + halo_ref[...].astype(F32)
    copy = pltpu.make_async_copy(total, out_ref.at[:, pl.ds(0, TAPS), :], sem)
    copy.start()
    copy.wait()


def join(grid, strip, halo):
    vmem = pl.BlockSpec(memory_space=pltpu.VMEM)
    whole = pl.BlockSpec(memory_space=pl.ANY)
    return pl.pallas_call(
        join_kernel,
        out_shape=jax.ShapeDtypeStruct(grid.shape, grid.dtype),
        in_specs=[whole, vmem, vmem],
        out_specs=whole,
        scratch_shapes=[pltpu.VMEM(strip.shape, F32), pltpu.SemaphoreType.DMA(())],
        input_output_aliases={0: 0},
        compiler_params=pltpu.CompilerParams(vmem_limit_bytes=2 << 20),
    )(grid, strip, halo)


def per_device(u_cell, v_cell, w_plane, counts, vis_values, kern_u, kern_v):
    n_fv = lax.axis_size("fv")
    n_fu = lax.axis_size("fu")
    rows = u_cell.shape[1]
    chans = vis_values.shape[0]
    width = 4096
    small = 80
    vis = vis_values[:, 0, :]
    kern_u, kern_v = kern_u.T, kern_v.T

    def exchange(cap):
        sent = pack(cap, n_fv, u_cell, v_cell, w_plane, counts, vis)
        return lax.all_to_all(sent, "fv", 0, 0)

    msgs = exchange(small)
    over = jnp.max(msgs[:, small // 2 + 4, 0]) > 0

    def whole():
        return border(rows, chans, exchange(rows), kern_u, kern_v, width)

    def usual():
        return border(small, chans, msgs, kern_u, kern_v, width)

    held, tiles, halo = lax.cond(over, whole, usual)
    came = lax.ppermute(halo, "fu", [(i, i + 1) for i in range(n_fu - 1)])
    grid, strip = main(tiles, held, kern_u, kern_v)
    return join(grid, strip, came)


def solution(mesh):
    return jax.shard_map(
        per_device,
        mesh=mesh,
        in_specs=(
            P("fu", "fv"),
            P("fu", "fv"),
            P("fu", "fv"),
            P("fu", "fv"),
            P("ch", "fu", "fv"),
            P(),
            P(),
        ),
        out_specs=P("ch", "fu", "fv"),
        check_vma=False,
    )
```

```python
import functools

import jax
import jax.numpy as jnp
from jax import lax
from jax.experimental import pallas as pl
from jax.experimental.pallas import tpu as pltpu
from jax.sharding import PartitionSpec as P

GU = 64
GV = 128
TAPS = 8
LANES = 128
META = 8
KT = 256
F32 = jnp.float32
BF16 = jnp.bfloat16
NT = (((1,), (1,)), ((), ()))


def tag_rows(half):
    per_row = LANES // (2 * META)
    return META * (-(-half // (META * per_row)))


def pack_kernel(
    half, n_dst, u_ref, v_ref, w_ref, counts_ref, vis_ref, kern_u_ref, kern_v_ref, out_ref, tables_ref, picks_s
):
    chans, rows = vis_ref.shape
    n_blocks = counts_ref.shape[1]
    block = rows // n_blocks
    cap = 2 * half
    tables_ref[:TAPS, :] = kern_u_ref[...]
    tables_ref[TAPS:, :] = kern_v_ref[...]
    u, v, w = u_ref[...], v_ref[...], w_ref[...]
    lane = lax.broadcasted_iota(jnp.int32, (1, rows), 1)
    limit = jnp.zeros((1, rows), jnp.int32)
    for b in range(n_blocks):
        limit = jnp.where(lane >= b * block, b * block + counts_ref[0, b], limit)
    live = lane < limit
    first = v // GV
    last = (v + (TAPS - 1)) // GV
    dst = lax.broadcasted_iota(jnp.int32, (n_dst, rows), 0)
    member = ((dst == first) | (dst == last)) & live
    member_f = member.astype(F32)
    before = lax.broadcasted_iota(jnp.int32, (rows, rows), 0) < lax.broadcasted_iota(
        jnp.int32, (rows, rows), 1
    )
    rank = jnp.dot(
        member_f.astype(BF16),
        before.astype(F32).astype(BF16),
        preferred_element_type=F32,
    )
    rank = jnp.where(member, rank.astype(jnp.int32), -1)
    total = jnp.sum(member_f, axis=1, keepdims=True)
    over = (jnp.max(total, axis=0, keepdims=True) > cap).astype(F32)
    tags = jnp.concatenate(
        [
            (u % GU).astype(F32),
            (v % GV).astype(F32),
            first.astype(F32),
            w.astype(F32),
            jnp.zeros((META - 4, rows), F32),
        ],
        axis=0,
    )
    empty = jnp.zeros_like(tags)
    tags = jnp.concatenate(
        [
            jnp.concatenate([tags, empty], axis=1),
            jnp.concatenate([empty, tags], axis=1),
            jnp.zeros((LANES - 2 * META, 2 * rows), F32),
        ],
        axis=0,
    ).astype(BF16)
    vis = vis_ref[...]
    blank = jnp.zeros_like(vis)
    source = jnp.concatenate(
        [
            jnp.concatenate([vis, blank], axis=1),
            jnp.concatenate([blank, vis], axis=1),
            tags,
        ],
        axis=0,
    )
    slot = lax.broadcasted_iota(jnp.int32, (cap, rows), 0)
    for d in range(n_dst):
        pick = (slot == rank[d : d + 1, :]).astype(F32).astype(BF16)
        picks_s[d * half : (d + 1) * half, :rows] = pick[:half]
        picks_s[d * half : (d + 1) * half, rows:] = pick[half:]
    sent = lax.dot_general(picks_s[...], source, NT, preferred_element_type=F32)
    out_ref[:, :half, :] = sent[:, :LANES].reshape(n_dst, half, LANES).astype(BF16)
    place = lax.broadcasted_iota(jnp.int32, (META, LANES), 1)
    per_row = LANES // (2 * META)
    for d in range(n_dst):
        held = jnp.minimum(total[d : d + 1, :], float(cap))
        coarse = jnp.floor(held / 64.0)
        row = jnp.where(place == 4, over, 0.0)
        row = jnp.where(place == 5, coarse, row)
        row = jnp.where(place == 6, held - 64.0 * coarse, row)
        for g in range(half // META):
            at = d * half + g * META
            part = sent[at : at + META, LANES:]
            shift = 2 * META * (g % per_row)
            row = row + (pltpu.roll(part, shift, 1) if shift else part)
            if g % per_row == per_row - 1 or g == half // META - 1:
                to = half + META * (g // per_row)
                out_ref[d, to : to + META, :] = row.astype(BF16)
                row = jnp.zeros((META, LANES), F32)


def pack(half, n_dst, u, v, w, counts, vis, kern_u, kern_v):
    vmem = pl.BlockSpec(memory_space=pltpu.VMEM)
    rows = u.shape[1]
    return pl.pallas_call(
        functools.partial(pack_kernel, half, n_dst),
        out_shape=(
            jax.ShapeDtypeStruct((n_dst, half + tag_rows(half), LANES), BF16),
            jax.ShapeDtypeStruct((2 * TAPS, kern_u.shape[1]), F32),
        ),
        in_specs=[vmem, vmem, vmem, pl.BlockSpec(memory_space=pltpu.SMEM), vmem, vmem, vmem],
        out_specs=(vmem, vmem),
        scratch_shapes=[pltpu.VMEM((n_dst * half, 2 * rows), BF16)],
        compiler_params=pltpu.CompilerParams(vmem_limit_bytes=(8 << 20) if half <= 64 else (24 << 20)),
    )(u, v, w, counts, vis, kern_u, kern_v)


def tap_rows(table, plane):
    result = jnp.zeros((TAPS, plane.shape[1]), F32)
    for p in range(table.shape[1]):
        result = jnp.where(plane == p, table[:, p : p + 1], result)
    return result


def spread(taps, start, low, span):
    cell = lax.broadcasted_iota(jnp.int32, (span, taps.shape[1]), 0) + (low - start)
    result = jnp.zeros((span, taps.shape[1]), F32)
    for t in range(TAPS):
        result = jnp.where(cell == t, taps[t : t + 1, :], result)
    return result


def v_weights(tags, plane, kern_v, facet):
    start = tags[1:2, :] + GV * (tags[2:3, :] - facet)
    wide = spread(tap_rows(kern_v, plane), start, 0, GV)
    high = wide.astype(BF16)
    low = (wide - high.astype(F32)).astype(BF16)
    return jnp.concatenate([high, low], axis=0)


def weighted(vis, ku):
    chans, span, lanes = vis.shape[0], ku.shape[0], vis.shape[1]
    full = vis[:, None, :] * ku[None, :, :]
    return full.reshape(chans * span, lanes).astype(BF16)


def border_kernel(half, chans, msgs_ref, tables_ref, held_ref, halo_ref, rows_s, acc):
    n_src = msgs_ref.shape[0]
    facet = lax.axis_index("fv")
    lane = lax.broadcasted_iota(jnp.int32, (META, LANES), 1)
    per_row = LANES // (2 * META)

    lengths = []
    for src in range(n_src):
        tags = msgs_ref[src, half : half + META, :].astype(F32)
        lengths.append((64.0 * tags[0, 5] + tags[0, 6]).astype(jnp.int32))

    def rows_of(src, upper):
        tags = msgs_ref[src, half:, :].astype(F32)
        vis = msgs_ref[src, :half, :].astype(F32)
        if upper:
            vis = pltpu.roll(vis, LANES // 2, 1)
        parts = []
        for g in range(half // META):
            at = META * (g // per_row)
            shift = (chans - 2 * META * (g % per_row) - META * upper) % LANES
            tag = pltpu.roll(tags[at : at + META], shift, 1)
            parts.append(jnp.where(lane < chans, vis[g * META : (g + 1) * META], tag))
        return jnp.concatenate(parts, axis=0)

    offset = 0
    for src in range(n_src):
        rows_s[pl.ds(offset, half), :] = rows_of(src, 0)

        @pl.when(lengths[src] > half)
        def _(src=src, offset=offset):
            rows_s[pl.ds(offset + half, half), :] = rows_of(src, 1)

        offset = offset + lengths[src]
    rows_s[pl.ds(offset, KT), :] = jnp.zeros((KT, LANES), F32)
    tiles = jnp.maximum((offset + KT - 1) // KT, 1)
    acc[...] = jnp.zeros_like(acc)
    kern_u, kern_v = tables_ref[:TAPS, :], tables_ref[TAPS:, :]
    tag_id = lax.broadcasted_iota(jnp.int32, (META, KT), 0)

    def step(k, _):
        cols = pl.ds(pl.multiple_of(k * KT, KT), KT)
        turned = rows_s[cols, :].T
        vis, tags = turned[:chans], turned[chans : chans + META]
        held_ref[:chans, cols] = vis.astype(BF16)
        held_ref[chans:, cols] = jnp.where(tag_id == META - 1, tiles.astype(F32), tags).astype(BF16)
        tags = tags.astype(jnp.int32)
        plane = tags[3:4, :]
        ku = spread(tap_rows(kern_u, plane), tags[0:1, :], GU, TAPS)
        left = weighted(vis, ku.astype(BF16).astype(F32))
        right = v_weights(tags, plane, kern_v, facet)
        acc[...] += lax.dot_general(left, right, NT, preferred_element_type=F32)
        return 0

    lax.fori_loop(0, tiles, step, 0)
    halo_ref[...] = (acc[:, :GV] + acc[:, GV:]).reshape(chans, TAPS, GV).astype(BF16)


def border(half, chans, msgs, tables, width):
    vmem = pl.BlockSpec(memory_space=pltpu.VMEM)
    return pl.pallas_call(
        functools.partial(border_kernel, half, chans),
        out_shape=(
            jax.ShapeDtypeStruct((chans + META, width), BF16),
            jax.ShapeDtypeStruct((chans, TAPS, GV), BF16),
        ),
        in_specs=[vmem, vmem],
        out_specs=(vmem, vmem),
        scratch_shapes=[
            pltpu.VMEM((width + 2 * KT, LANES), F32),
            pltpu.VMEM((chans * TAPS, 2 * GV), F32),
        ],
        compiler_params=pltpu.CompilerParams(vmem_limit_bytes=12 << 20),
    )(msgs, tables)


def main_kernel(step_chans, held_ref, tables_ref, out_ref, strip_ref, grid_s, ku_s, kv_s, acc, sems):
    chans = held_ref.shape[0] - META
    facet = lax.axis_index("fv")
    kern_u, kern_v = tables_ref[:TAPS, :], tables_ref[TAPS:, :]
    tiles = held_ref[chans:, :LANES].astype(F32)[META - 1, 0].astype(jnp.int32)

    def prepare(k):
        cols = pl.ds(pl.multiple_of(k * KT, KT), KT)
        tags = held_ref[chans:, cols].astype(F32).astype(jnp.int32)
        plane = tags[3:4, :]
        ku_s[:, cols] = spread(tap_rows(kern_u, plane), tags[0:1, :], 0, GU).astype(BF16)
        start = tags[1:2, :] + GV * (tags[2:3, :] - facet)
        wide = spread(tap_rows(kern_v, plane), start, 0, GV).T
        high = wide.astype(BF16)
        kv_s[cols, :GV] = high
        kv_s[cols, GV:] = (wide - high.astype(F32)).astype(BF16)

    def product(first, cols):
        vis = held_ref[pl.ds(first, step_chans), cols].astype(F32)
        left = weighted(vis, ku_s[:, cols].astype(F32))
        return jnp.dot(left, kv_s[cols, :], preferred_element_type=F32)

    def copy_out(i):
        some = pl.ds(i * step_chans, step_chans)
        return pltpu.make_async_copy(grid_s.at[some], out_ref.at[some], sems.at[i])

    def emit(i, total):
        total = (total[:, :GV] + total[:, GV:]).reshape(step_chans, GU, GV)
        some = pl.ds(i * step_chans, step_chans)
        grid_s[some] = total
        strip_ref[some] = total[:, :TAPS, :]
        copy_out(i).start()

    steps = chans // step_chans
    for n in (1, 2, 3):

        @pl.when(tiles == n)
        def _(n=n):
            for k in range(n):
                prepare(k)
            for i in range(steps):
                emit(i, product(i * step_chans, pl.ds(0, n * KT)))

    @pl.when(tiles > 3)
    def _():
        lax.fori_loop(0, tiles, lambda k, _: (prepare(k), 0)[1], 0)
        for i in range(steps):
            acc[...] = jnp.zeros_like(acc)

            def step(k, _, i=i):
                acc[...] += product(i * step_chans, pl.ds(pl.multiple_of(k * KT, KT), KT))
                return 0

            lax.fori_loop(0, tiles, step, 0)
            emit(i, acc[...])

    for i in range(steps):
        copy_out(i).wait()


def main(held, tables, step_chans=16):
    depth, width = held.shape
    chans = depth - META
    vmem = pl.BlockSpec(memory_space=pltpu.VMEM)
    return pl.pallas_call(
        functools.partial(main_kernel, step_chans),
        out_shape=(
            jax.ShapeDtypeStruct((chans, GU, GV), F32),
            jax.ShapeDtypeStruct((chans, TAPS, GV), F32),
        ),
        in_specs=[vmem, vmem],
        out_specs=(pl.BlockSpec(memory_space=pl.ANY), vmem),
        scratch_shapes=[
            pltpu.VMEM((chans, GU, GV), F32),
            pltpu.VMEM((GU, width), BF16),
            pltpu.VMEM((width, 2 * GV), BF16),
            pltpu.VMEM((step_chans * GU, 2 * GV), F32),
            pltpu.SemaphoreType.DMA((chans // step_chans,)),
        ],
        compiler_params=pltpu.CompilerParams(vmem_limit_bytes=18 << 20),
    )(held, tables)


def join_kernel(_, strip_ref, halo_ref, out_ref, total, sem):
    total[...] = strip_ref[...] + halo_ref[...].astype(F32)
    copy = pltpu.make_async_copy(total, out_ref.at[:, pl.ds(0, TAPS), :], sem)
    copy.start()
    copy.wait()


def join(grid, strip, halo):
    vmem = pl.BlockSpec(memory_space=pltpu.VMEM)
    whole = pl.BlockSpec(memory_space=pl.ANY)
    return pl.pallas_call(
        join_kernel,
        out_shape=jax.ShapeDtypeStruct(grid.shape, grid.dtype),
        in_specs=[whole, vmem, vmem],
        out_specs=whole,
        scratch_shapes=[pltpu.VMEM(strip.shape, F32), pltpu.SemaphoreType.DMA(())],
        input_output_aliases={0: 0},
        compiler_params=pltpu.CompilerParams(vmem_limit_bytes=2 << 20),
    )(grid, strip, halo)


def per_device(u_cell, v_cell, w_plane, counts, vis_values, kern_u, kern_v):
    n_fv = lax.axis_size("fv")
    n_fu = lax.axis_size("fu")
    rows = u_cell.shape[1]
    chans = vis_values.shape[0]
    width = 4096
    usual_half = 40
    vis = vis_values[:, 0, :]

    def exchange(half):
        sent, tables = pack(half, n_fv, u_cell, v_cell, w_plane, counts, vis, kern_u.T, kern_v.T)
        return lax.all_to_all(sent, "fv", 0, 0), tables

    msgs, tables = exchange(usual_half)
    over = jnp.any(msgs[:, usual_half, 4] > 0)

    def whole():
        return border(rows // 2, chans, exchange(rows // 2)[0], tables, width)

    def usual():
        return border(usual_half, chans, msgs, tables, width)

    held, halo = lax.cond(over, whole, usual)
    came = lax.ppermute(halo, "fu", [(i, i + 1) for i in range(n_fu - 1)])
    grid, strip = main(held, tables)
    return join(grid, strip, came)


def solution(mesh):
    return jax.shard_map(
        per_device,
        mesh=mesh,
        in_specs=(
            P("fu", "fv"),
            P("fu", "fv"),
            P("fu", "fv"),
            P("fu", "fv"),
            P("ch", "fu", "fv"),
            P(),
            P(),
        ),
        out_specs=P("ch", "fu", "fv"),
        check_vma=False,
    )
```

```python
import functools

import jax
import jax.numpy as jnp
from jax import lax
from jax.experimental import pallas as pl
from jax.experimental.pallas import tpu as pltpu
from jax.sharding import PartitionSpec as P

GU = 64
GV = 128
TAPS = 8
LANES = 128
META = 8
KT = 256
F32 = jnp.float32
BF16 = jnp.bfloat16
NT = (((1,), (1,)), ((), ()))


def tag_rows(half):
    per_row = LANES // (2 * META)
    return META * (-(-half // (META * per_row)))


def pack_kernel(
    half, n_dst, u_ref, v_ref, w_ref, counts_ref, vis_ref, kern_u_ref, kern_v_ref, out_ref, tables_ref, picks_s
):
    chans, rows = vis_ref.shape
    n_blocks = counts_ref.shape[1]
    block = rows // n_blocks
    cap = 2 * half
    tables_ref[:TAPS, :] = kern_u_ref[...]
    tables_ref[TAPS:, :] = kern_v_ref[...]
    u, v, w = u_ref[...], v_ref[...], w_ref[...]
    lane = lax.broadcasted_iota(jnp.int32, (1, rows), 1)
    limit = jnp.zeros((1, rows), jnp.int32)
    for b in range(n_blocks):
        limit = jnp.where(lane >= b * block, b * block + counts_ref[0, b], limit)
    live = lane < limit
    first = v // GV
    last = (v + (TAPS - 1)) // GV
    dst = lax.broadcasted_iota(jnp.int32, (n_dst, rows), 0)
    member = ((dst == first) | (dst == last)) & live
    member_f = member.astype(F32)
    before = lax.broadcasted_iota(jnp.int32, (rows, rows), 0) < lax.broadcasted_iota(
        jnp.int32, (rows, rows), 1
    )
    rank = jnp.dot(
        member_f.astype(BF16),
        before.astype(F32).astype(BF16),
        preferred_element_type=F32,
    )
    rank = jnp.where(member, rank.astype(jnp.int32), -1)
    total = jnp.sum(member_f, axis=1, keepdims=True)
    over = (jnp.max(total, axis=0, keepdims=True) > cap).astype(F32)
    tags = jnp.concatenate(
        [
            (u % GU).astype(F32),
            (v % GV).astype(F32),
            first.astype(F32),
            w.astype(F32),
            jnp.zeros((META - 4, rows), F32),
        ],
        axis=0,
    )
    empty = jnp.zeros_like(tags)
    tags = jnp.concatenate(
        [
            jnp.concatenate([tags, empty], axis=1),
            jnp.concatenate([empty, tags], axis=1),
            jnp.zeros((LANES - 2 * META, 2 * rows), F32),
        ],
        axis=0,
    ).astype(BF16)
    vis = vis_ref[...]
    blank = jnp.zeros_like(vis)
    source = jnp.concatenate(
        [
            jnp.concatenate([vis, blank], axis=1),
            jnp.concatenate([blank, vis], axis=1),
            tags,
        ],
        axis=0,
    )
    slot = lax.broadcasted_iota(jnp.int32, (cap, rows), 0)
    for d in range(n_dst):
        pick = (slot == rank[d : d + 1, :]).astype(F32).astype(BF16)
        picks_s[d * half : (d + 1) * half, :rows] = pick[:half]
        picks_s[d * half : (d + 1) * half, rows:] = pick[half:]
    sent = lax.dot_general(picks_s[...], source, NT, preferred_element_type=F32)
    out_ref[:, :half, :] = sent[:, :LANES].reshape(n_dst, half, LANES).astype(BF16)
    place = lax.broadcasted_iota(jnp.int32, (META, LANES), 1)
    per_row = LANES // (2 * META)
    for d in range(n_dst):
        eights = jnp.floor((jnp.minimum(total[d : d + 1, :], float(cap)) + (META - 1)) / META)
        row = jnp.where(place == 4, over, 0.0)
        row = jnp.where(place == 5, eights, row)
        for g in range(half // META):
            at = d * half + g * META
            part = sent[at : at + META, LANES:]
            shift = 2 * META * (g % per_row)
            row = row + (pltpu.roll(part, shift, 1) if shift else part)
            if g % per_row == per_row - 1 or g == half // META - 1:
                to = half + META * (g // per_row)
                out_ref[d, to : to + META, :] = row.astype(BF16)
                row = jnp.zeros((META, LANES), F32)


def pack(half, n_dst, u, v, w, counts, vis, kern_u, kern_v):
    vmem = pl.BlockSpec(memory_space=pltpu.VMEM)
    rows = u.shape[1]
    return pl.pallas_call(
        functools.partial(pack_kernel, half, n_dst),
        out_shape=(
            jax.ShapeDtypeStruct((n_dst, half + tag_rows(half), LANES), BF16),
            jax.ShapeDtypeStruct((2 * TAPS, kern_u.shape[1]), F32),
        ),
        in_specs=[vmem, vmem, vmem, pl.BlockSpec(memory_space=pltpu.SMEM), vmem, vmem, vmem],
        out_specs=(vmem, vmem),
        scratch_shapes=[pltpu.VMEM((n_dst * half, 2 * rows), BF16)],
        compiler_params=pltpu.CompilerParams(vmem_limit_bytes=(8 << 20) if half <= 64 else (24 << 20)),
    )(u, v, w, counts, vis, kern_u, kern_v)


def tap_rows(table, plane):
    result = jnp.zeros((TAPS, plane.shape[1]), F32)
    for p in range(table.shape[1]):
        result = jnp.where(plane == p, table[:, p : p + 1], result)
    return result


def spread(taps, start, low, span):
    cell = lax.broadcasted_iota(jnp.int32, (span, taps.shape[1]), 0) + (low - start)
    result = jnp.zeros((span, taps.shape[1]), F32)
    for t in range(TAPS):
        result = jnp.where(cell == t, taps[t : t + 1, :], result)
    return result


def weighted(vis, ku):
    chans, span, lanes = vis.shape[0], ku.shape[0], vis.shape[1]
    full = vis[:, None, :] * ku[None, :, :]
    return full.reshape(chans * span, lanes).astype(BF16)


def border_kernel(half, chans, msgs_ref, tables_ref, held_ref, halo_ref, over_ref, *rest):
    rows_s, acc = rest[-2:]
    n_src = msgs_ref.shape[0]
    facet = lax.axis_index("fv")
    lane = lax.broadcasted_iota(jnp.int32, (META, LANES), 1)
    per_row = LANES // (2 * META)

    lengths = []
    over = jnp.zeros((META, LANES), F32)
    for src in range(n_src):
        tags = msgs_ref[src, half : half + META, :].astype(F32)
        over = over + tags
        lengths.append(tags[0, 5].astype(jnp.int32) * META)

    def rows_of(src, upper):
        tags = msgs_ref[src, half:, :].astype(F32)
        vis = msgs_ref[src, :half, :].astype(F32)
        if upper:
            vis = pltpu.roll(vis, LANES // 2, 1)
        parts = []
        for g in range(half // META):
            at = META * (g // per_row)
            shift = (chans - 2 * META * (g % per_row) - META * upper) % LANES
            tag = pltpu.roll(tags[at : at + META], shift, 1)
            parts.append(jnp.where(lane < chans, vis[g * META : (g + 1) * META], tag))
        return jnp.concatenate(parts, axis=0)

    over = over[0, 4].astype(jnp.int32)
    over_ref[0, 0] = over
    offset = 0
    for src in range(n_src):
        rows_s[pl.ds(offset, half), :] = rows_of(src, 0)

        @pl.when(lengths[src] > half)
        def _(src=src, offset=offset):
            rows_s[pl.ds(offset + half, half), :] = rows_of(src, 1)

        offset = pl.multiple_of(offset + lengths[src], META)
    rows_s[pl.ds(offset, KT), :] = jnp.zeros((KT, LANES), F32)
    tiles = jnp.maximum((offset + KT - 1) // KT, 1)
    kern_u, kern_v = tables_ref[:TAPS, :], tables_ref[TAPS:, :]
    tag_id = lax.broadcasted_iota(jnp.int32, (META, KT), 0)
    kept = jnp.where(over > 0, 0, tiles).astype(F32)

    def operands(k):
        cols = pl.ds(pl.multiple_of(k * KT, KT), KT)
        turned = rows_s[cols, :].T
        vis, tags = turned[:chans], turned[chans : chans + META]
        held_ref[:chans, cols] = vis.astype(BF16)
        held_ref[chans:, cols] = jnp.where(tag_id == META - 1, kept, tags).astype(BF16)
        tags = tags.astype(jnp.int32)
        plane = tags[3:4, :]
        ku = spread(tap_rows(kern_u, plane), tags[0:1, :], GU, TAPS)
        left = weighted(vis, ku.astype(BF16).astype(F32))
        start = tags[1:2, :] + GV * (tags[2:3, :] - facet)
        return left, spread(tap_rows(kern_v, plane), start, 0, GV).astype(BF16)

    def emit(total):
        halo_ref[...] = total.reshape(chans, TAPS, GV).astype(BF16)

    for n in (1, 2, 3):

        @pl.when(tiles == n)
        def _(n=n):
            pairs = [operands(k) for k in range(n)]
            left = jnp.concatenate([p[0] for p in pairs], axis=1)
            right = jnp.concatenate([p[1] for p in pairs], axis=1)
            emit(lax.dot_general(left, right, NT, preferred_element_type=F32))

    @pl.when(tiles > 3)
    def _():
        acc[...] = jnp.zeros_like(acc)

        def step(k, _):
            left, right = operands(k)
            acc[...] += lax.dot_general(left, right, NT, preferred_element_type=F32)
            return 0

        lax.fori_loop(0, tiles, step, 0)
        emit(acc[...])


def border(half, chans, msgs, tables, width, spare):
    vmem = pl.BlockSpec(memory_space=pltpu.VMEM)
    return pl.pallas_call(
        functools.partial(border_kernel, half, chans),
        out_shape=(
            jax.ShapeDtypeStruct((chans + META, width), BF16),
            jax.ShapeDtypeStruct((chans, TAPS, GV), BF16),
            jax.ShapeDtypeStruct((1, 1), jnp.int32),
        )
        + (jax.ShapeDtypeStruct((chans + META, width), BF16),) * spare,
        in_specs=[vmem, vmem],
        out_specs=(vmem, vmem, pl.BlockSpec(memory_space=pltpu.SMEM))
        + (pl.BlockSpec(memory_space=pl.ANY),) * spare,
        scratch_shapes=[
            pltpu.VMEM((width + 2 * KT, LANES), F32),
            pltpu.VMEM((chans * TAPS, GV), F32),
        ],
        compiler_params=pltpu.CompilerParams(vmem_limit_bytes=12 << 20),
    )(msgs, tables)


def main_kernel(
    step_chans, held_ref, other_ref, tables_ref, out_ref, strip_ref, other_s, grid_s, ku_s, kv_s, acc, sems, other_sem
):
    chans = held_ref.shape[0] - META
    facet = lax.axis_index("fv")
    kern_u, kern_v = tables_ref[:TAPS, :], tables_ref[TAPS:, :]

    def tiles_of(ref):
        return ref[chans:, :LANES].astype(F32)[META - 1, 0].astype(jnp.int32)

    def prepare(ref, k):
        cols = pl.ds(pl.multiple_of(k * KT, KT), KT)
        tags = ref[chans:, cols].astype(F32).astype(jnp.int32)
        plane = tags[3:4, :]
        ku_s[:, cols] = spread(tap_rows(kern_u, plane), tags[0:1, :], 0, GU).astype(BF16)
        start = tags[1:2, :] + GV * (tags[2:3, :] - facet)
        wide = spread(tap_rows(kern_v, plane), start, 0, GV).T
        high = wide.astype(BF16)
        kv_s[cols, :GV] = high
        kv_s[cols, GV:] = (wide - high.astype(F32)).astype(BF16)

    def product(ref, first, cols):
        vis = ref[pl.ds(first, step_chans), cols].astype(F32)
        left = weighted(vis, ku_s[:, cols].astype(F32))
        return jnp.dot(left, kv_s[cols, :], preferred_element_type=F32)

    def copy_out(i):
        some = pl.ds(i * step_chans, step_chans)
        return pltpu.make_async_copy(grid_s.at[some], out_ref.at[some], sems.at[i])

    def emit(i, total):
        total = (total[:, :GV] + total[:, GV:]).reshape(step_chans, GU, GV)
        some = pl.ds(i * step_chans, step_chans)
        grid_s[some] = total
        strip_ref[some] = total[:, :TAPS, :]
        copy_out(i).start()

    steps = chans // step_chans
    tiles = tiles_of(held_ref)

    def any_count(ref, count):
        lax.fori_loop(0, count, lambda k, _: (prepare(ref, k), 0)[1], 0)
        for i in range(steps):
            acc[...] = jnp.zeros_like(acc)

            def step(k, _, i=i):
                acc[...] += product(ref, i * step_chans, pl.ds(pl.multiple_of(k * KT, KT), KT))
                return 0

            lax.fori_loop(0, count, step, 0)
            emit(i, acc[...])

    for n in (1, 2, 3):

        @pl.when(tiles == n)
        def _(n=n):
            for k in range(n):
                prepare(held_ref, k)
            for i in range(steps):
                emit(i, product(held_ref, i * step_chans, pl.ds(0, n * KT)))

    @pl.when(tiles > 3)
    def _():
        any_count(held_ref, tiles)

    @pl.when(tiles == 0)
    def _():
        fetch = pltpu.make_async_copy(other_ref, other_s, other_sem)
        fetch.start()
        fetch.wait()
        any_count(other_s, tiles_of(other_s))

    for i in range(steps):
        copy_out(i).wait()


def main(held, other, tables, step_chans=16):
    depth, width = held.shape
    chans = depth - META
    vmem = pl.BlockSpec(memory_space=pltpu.VMEM)
    return pl.pallas_call(
        functools.partial(main_kernel, step_chans),
        out_shape=(
            jax.ShapeDtypeStruct((chans, GU, GV), F32),
            jax.ShapeDtypeStruct((chans, TAPS, GV), F32),
        ),
        in_specs=[vmem, pl.BlockSpec(memory_space=pl.ANY), vmem],
        out_specs=(pl.BlockSpec(memory_space=pl.ANY), vmem),
        scratch_shapes=[
            pltpu.VMEM(held.shape, BF16),
            pltpu.VMEM((chans, GU, GV), F32),
            pltpu.VMEM((GU, width), BF16),
            pltpu.VMEM((width, 2 * GV), BF16),
            pltpu.VMEM((step_chans * GU, 2 * GV), F32),
            pltpu.SemaphoreType.DMA((chans // step_chans,)),
            pltpu.SemaphoreType.DMA(()),
        ],
        compiler_params=pltpu.CompilerParams(vmem_limit_bytes=18 << 20),
    )(held, other, tables)


def join_kernel(_, strip_ref, halo_ref, out_ref, total, sem):
    below = jnp.where(lax.axis_index("fu") > 0, halo_ref[...].astype(F32), 0.0)
    total[...] = strip_ref[...] + below
    copy = pltpu.make_async_copy(total, out_ref.at[:, pl.ds(0, TAPS), :], sem)
    copy.start()
    copy.wait()


def join(grid, strip, halo):
    vmem = pl.BlockSpec(memory_space=pltpu.VMEM)
    whole = pl.BlockSpec(memory_space=pl.ANY)
    return pl.pallas_call(
        join_kernel,
        out_shape=jax.ShapeDtypeStruct(grid.shape, grid.dtype),
        in_specs=[whole, vmem, vmem],
        out_specs=whole,
        scratch_shapes=[pltpu.VMEM(strip.shape, F32), pltpu.SemaphoreType.DMA(())],
        input_output_aliases={0: 0},
        compiler_params=pltpu.CompilerParams(vmem_limit_bytes=2 << 20),
    )(grid, strip, halo)


def per_device(u_cell, v_cell, w_plane, counts, vis_values, kern_u, kern_v):
    n_fv = lax.axis_size("fv")
    n_fu = lax.axis_size("fu")
    rows = u_cell.shape[1]
    chans = vis_values.shape[0]
    width = 4096
    usual_half = 40
    vis = vis_values[:, 0, :]

    def exchange(half):
        sent, tables = pack(half, n_fv, u_cell, v_cell, w_plane, counts, vis, kern_u.T, kern_v.T)
        return lax.all_to_all(sent, "fv", 0, 0), tables

    msgs, tables = exchange(usual_half)
    held, halo, over, other = border(usual_half, chans, msgs, tables, width, 1)

    def whole(_):
        return border(rows // 2, chans, exchange(rows // 2)[0], tables, width, 0)

    other, halo, _ = lax.while_loop(lambda state: state[2][0, 0] > 0, whole, (other, halo, over))
    came = lax.ppermute(halo, "fu", [(i, (i + 1) % n_fu) for i in range(n_fu)])
    grid, strip = main(held, other, tables)
    return join(grid, strip, came)


def solution(mesh):
    return jax.shard_map(
        per_device,
        mesh=mesh,
        in_specs=(
            P("fu", "fv"),
            P("fu", "fv"),
            P("fu", "fv"),
            P("fu", "fv"),
            P("ch", "fu", "fv"),
            P(),
            P(),
        ),
        out_specs=P("ch", "fu", "fv"),
        check_vma=False,
    )
```

```python
import functools

import jax
import jax.numpy as jnp
from jax import lax
from jax.experimental import pallas as pl
from jax.experimental.pallas import tpu as pltpu
from jax.sharding import PartitionSpec as P

GU = 64
GV = 128
TAPS = 8
LANES = 128
META = 8
KT = 256
F32 = jnp.float32
BF16 = jnp.bfloat16
NT = (((1,), (1,)), ((), ()))


def tag_rows(half):
    per_row = LANES // (2 * META)
    return META * (-(-half // (META * per_row)))


def pack_kernel(
    half, n_dst, u_ref, v_ref, w_ref, counts_ref, vis_ref, kern_u_ref, kern_v_ref, out_ref, tables_ref, picks_s
):
    chans, rows = vis_ref.shape
    n_blocks = counts_ref.shape[1]
    block = rows // n_blocks
    cap = 2 * half
    tables_ref[:TAPS, :] = kern_u_ref[...]
    tables_ref[TAPS:, :] = kern_v_ref[...]
    u, v, w = u_ref[...], v_ref[...], w_ref[...]
    lane = lax.broadcasted_iota(jnp.int32, (1, rows), 1)
    limit = jnp.zeros((1, rows), jnp.int32)
    for b in range(n_blocks):
        limit = jnp.where(lane >= b * block, b * block + counts_ref[0, b], limit)
    live = lane < limit
    first = v // GV
    last = (v + (TAPS - 1)) // GV
    dst = lax.broadcasted_iota(jnp.int32, (n_dst, rows), 0)
    member = ((dst == first) | (dst == last)) & live
    edge = member & (u % GU > GU - TAPS)
    plain_f = (member & jnp.logical_not(edge)).astype(F32)
    edge_f = edge.astype(F32)
    before = lax.broadcasted_iota(jnp.int32, (rows, rows), 0) < lax.broadcasted_iota(
        jnp.int32, (rows, rows), 1
    )
    rank = jnp.dot(
        jnp.concatenate([edge_f, plain_f], axis=0).astype(BF16),
        before.astype(F32).astype(BF16),
        preferred_element_type=F32,
    )
    edges = jnp.sum(edge_f, axis=1, keepdims=True)
    total = edges + jnp.sum(plain_f, axis=1, keepdims=True)
    rank = jnp.where(edge, rank[:n_dst], rank[n_dst:] + edges)
    rank = jnp.where(member, rank.astype(jnp.int32), -1)
    over = (jnp.max(total, axis=0, keepdims=True) > cap).astype(F32)
    tags = jnp.concatenate(
        [
            (u % GU).astype(F32),
            (v % GV).astype(F32),
            first.astype(F32),
            w.astype(F32),
            jnp.zeros((META - 4, rows), F32),
        ],
        axis=0,
    )
    empty = jnp.zeros_like(tags)
    tags = jnp.concatenate(
        [
            jnp.concatenate([tags, empty], axis=1),
            jnp.concatenate([empty, tags], axis=1),
            jnp.zeros((LANES - 2 * META, 2 * rows), F32),
        ],
        axis=0,
    ).astype(BF16)
    vis = vis_ref[...]
    blank = jnp.zeros_like(vis)
    source = jnp.concatenate(
        [
            jnp.concatenate([vis, blank], axis=1),
            jnp.concatenate([blank, vis], axis=1),
            tags,
        ],
        axis=0,
    )
    slot = lax.broadcasted_iota(jnp.int32, (cap, rows), 0)
    for d in range(n_dst):
        pick = (slot == rank[d : d + 1, :]).astype(F32).astype(BF16)
        picks_s[d * half : (d + 1) * half, :rows] = pick[:half]
        picks_s[d * half : (d + 1) * half, rows:] = pick[half:]
    sent = lax.dot_general(picks_s[...], source, NT, preferred_element_type=F32)
    out_ref[:, :half, :] = sent[:, :LANES].reshape(n_dst, half, LANES).astype(BF16)
    place = lax.broadcasted_iota(jnp.int32, (META, LANES), 1)
    per_row = LANES // (2 * META)
    for d in range(n_dst):
        eights = jnp.floor((jnp.minimum(total[d : d + 1, :], float(cap)) + (META - 1)) / META)
        row = jnp.where(place == 4, over, 0.0)
        row = jnp.where(place == 5, eights, row)
        row = jnp.where(place == 6, jnp.floor((edges[d : d + 1, :] + (META - 1)) / META), row)
        for g in range(half // META):
            at = d * half + g * META
            part = sent[at : at + META, LANES:]
            shift = 2 * META * (g % per_row)
            row = row + (pltpu.roll(part, shift, 1) if shift else part)
            if g % per_row == per_row - 1 or g == half // META - 1:
                to = half + META * (g // per_row)
                out_ref[d, to : to + META, :] = row.astype(BF16)
                row = jnp.zeros((META, LANES), F32)


def pack(half, n_dst, u, v, w, counts, vis, kern_u, kern_v):
    vmem = pl.BlockSpec(memory_space=pltpu.VMEM)
    rows = u.shape[1]
    return pl.pallas_call(
        functools.partial(pack_kernel, half, n_dst),
        out_shape=(
            jax.ShapeDtypeStruct((n_dst, half + tag_rows(half), LANES), BF16),
            jax.ShapeDtypeStruct((2 * TAPS, kern_u.shape[1]), F32),
        ),
        in_specs=[vmem, vmem, vmem, pl.BlockSpec(memory_space=pltpu.SMEM), vmem, vmem, vmem],
        out_specs=(vmem, vmem),
        scratch_shapes=[pltpu.VMEM((n_dst * half, 2 * rows), BF16)],
        compiler_params=pltpu.CompilerParams(vmem_limit_bytes=(8 << 20) if half <= 64 else (24 << 20)),
    )(u, v, w, counts, vis, kern_u, kern_v)


def tap_rows(table, plane):
    result = jnp.zeros((TAPS, plane.shape[1]), F32)
    for p in range(table.shape[1]):
        result = jnp.where(plane == p, table[:, p : p + 1], result)
    return result


def spread(taps, start, low, span):
    cell = lax.broadcasted_iota(jnp.int32, (span, taps.shape[1]), 0) + (low - start)
    result = jnp.zeros((span, taps.shape[1]), F32)
    for t in range(TAPS):
        result = jnp.where(cell == t, taps[t : t + 1, :], result)
    return result


def weighted(vis, ku):
    chans, span, lanes = vis.shape[0], ku.shape[0], vis.shape[1]
    full = vis[:, None, :] * ku[None, :, :]
    return full.reshape(chans * span, lanes).astype(BF16)


def merged_rows(half, chans, msgs_ref, src, upper, groups):
    lane = lax.broadcasted_iota(jnp.int32, (META, LANES), 1)
    per_row = LANES // (2 * META)
    parts = []
    for g in groups:
        at = half + META * (g // per_row)
        vis = msgs_ref[src, g * META : (g + 1) * META, :].astype(F32)
        tag = msgs_ref[src, at : at + META, :].astype(F32)
        if upper:
            vis = pltpu.roll(vis, LANES // 2, 1)
        shift = (chans - 2 * META * (g % per_row) - META * upper) % LANES
        parts.append(jnp.where(lane < chans, vis, pltpu.roll(tag, shift, 1)))
    return jnp.concatenate(parts, axis=0)


def gather_rows(half, chans, msgs_ref, rows_s):
    n_src = msgs_ref.shape[0]
    groups = range(half // META)
    lengths = []
    for src in range(n_src):
        tags = msgs_ref[src, half : half + META, :].astype(F32)
        lengths.append(tags[0, 5].astype(jnp.int32) * META)
    offset = 0
    for src in range(n_src):
        rows_s[pl.ds(offset, half), :] = merged_rows(half, chans, msgs_ref, src, 0, groups)

        @pl.when(lengths[src] > half)
        def _(src=src, offset=offset):
            rows_s[pl.ds(offset + half, half), :] = merged_rows(half, chans, msgs_ref, src, 1, groups)

        offset = pl.multiple_of(offset + lengths[src], META)
    rows_s[pl.ds(offset, KT), :] = jnp.zeros((KT, LANES), F32)
    return jnp.maximum((offset + KT - 1) // KT, 1)


def turn_tile(chans, rows_s, held, tiles, k):
    cols = pl.ds(pl.multiple_of(k * KT, KT), KT)
    turned = rows_s[cols, :].T
    tag_id = lax.broadcasted_iota(jnp.int32, (META, KT), 0)
    tags = turned[chans : chans + META]
    held[:chans, cols] = turned[:chans].astype(BF16)
    held[chans:, cols] = jnp.where(tag_id == META - 1, tiles.astype(F32), tags).astype(BF16)


def border_product(chans, block, tables_ref):
    kern_u, kern_v = tables_ref[:TAPS, :], tables_ref[TAPS:, :]
    turned = block.T
    tags = turned[chans : chans + META].astype(jnp.int32)
    plane = tags[3:4, :]
    ku = spread(tap_rows(kern_u, plane), tags[0:1, :], GU, TAPS)
    left = weighted(turned[:chans], ku.astype(BF16).astype(F32))
    start = tags[1:2, :] + GV * (tags[2:3, :] - lax.axis_index("fv"))
    right = spread(tap_rows(kern_v, plane), start, 0, GV).astype(BF16)
    return lax.dot_general(left, right, NT, preferred_element_type=F32)


def sum_of_tags(half, msgs_ref):
    total = jnp.zeros((META, LANES), F32)
    for src in range(msgs_ref.shape[0]):
        total = total + msgs_ref[src, half : half + META, :].astype(F32)
    return total


def whole_kernel(half, chans, msgs_ref, tables_ref, held_ref, halo_ref, over_ref, rows_s, acc):
    tiles = gather_rows(half, chans, msgs_ref, rows_s)
    acc[...] = jnp.zeros_like(acc)

    def step(k, _):
        turn_tile(chans, rows_s, held_ref, tiles, k)
        block = rows_s[pl.ds(pl.multiple_of(k * KT, KT), KT), :]
        acc[...] += border_product(chans, block, tables_ref)
        return 0

    lax.fori_loop(0, tiles, step, 0)
    halo_ref[...] = acc[...].reshape(chans, TAPS, GV).astype(BF16)
    over_ref[0, 0] = 0


def early():
    return lax.axis_index("fu") % 2 == 1


def usual_kernel(half, chans, msgs_ref, tables_ref, held_ref, halo_ref, over_ref, other_ref, rows_s, acc):
    n_src = msgs_ref.shape[0]
    groups = half // META
    over_ref[0, 0] = sum_of_tags(half, msgs_ref)[0, 4].astype(jnp.int32)
    most = jnp.zeros((META, LANES), F32)
    for src in range(n_src):
        most = jnp.maximum(most, msgs_ref[src, half : half + META, :].astype(F32))
    chunks = most[0, 6].astype(jnp.int32)

    def chunk(c):
        upper, g = c // groups, c % groups
        block = [merged_rows(half, chans, msgs_ref, src, upper, [g]) for src in range(n_src)]
        return border_product(chans, jnp.concatenate(block, axis=0), tables_ref)

    def emit(total):
        halo_ref[...] = total.reshape(chans, TAPS, GV).astype(BF16)

    @pl.when(chunks <= 1)
    def _():
        emit(chunk(0))

    @pl.when(chunks > 1)
    def _():
        acc[...] = chunk(0) + chunk(1)
        for c in range(2, 2 * groups):

            @pl.when(chunks > c)
            def _(c=c):
                acc[...] += chunk(c)

        emit(acc[...])

    @pl.when(early())
    def _():
        tiles = gather_rows(half, chans, msgs_ref, rows_s)
        lax.fori_loop(0, tiles, lambda k, _: (turn_tile(chans, rows_s, held_ref, tiles, k), 0)[1], 0)


def border(half, chans, msgs, tables, width, usual):
    vmem = pl.BlockSpec(memory_space=pltpu.VMEM)
    whole = jax.ShapeDtypeStruct((chans + META, width), BF16)
    most = width
    if usual:
        most = -(-2 * half * msgs.shape[0] // KT) * KT
    return pl.pallas_call(
        functools.partial(usual_kernel if usual else whole_kernel, half, chans),
        out_shape=(
            jax.ShapeDtypeStruct((chans + META, most), BF16),
            jax.ShapeDtypeStruct((chans, TAPS, GV), BF16),
            jax.ShapeDtypeStruct((1, 1), jnp.int32),
        )
        + (whole,) * usual,
        in_specs=[vmem, vmem],
        out_specs=(vmem, vmem, pl.BlockSpec(memory_space=pltpu.SMEM))
        + (pl.BlockSpec(memory_space=pl.ANY),) * usual,
        scratch_shapes=[
            pltpu.VMEM((most + 2 * KT, LANES), F32),
            pltpu.VMEM((chans * TAPS, GV), F32),
        ],
        compiler_params=pltpu.CompilerParams(vmem_limit_bytes=12 << 20),
    )(msgs, tables)


def main_kernel(
    half, step_chans, msgs_ref, held_ref, other_ref, tables_ref, out_ref, strip_ref,
    held_s, rows_s, grid_s, ku_s, kv_s, acc, sems, other_sem, tiles_s
):
    chans = held_s.shape[0] - META
    facet = lax.axis_index("fv")
    kern_u, kern_v = tables_ref[:TAPS, :], tables_ref[TAPS:, :]

    def tiles_of(ref):
        return ref[chans:, :LANES].astype(F32)[META - 1, 0].astype(jnp.int32)

    def prepare(k):
        cols = pl.ds(pl.multiple_of(k * KT, KT), KT)
        tags = held_s[chans:, cols].astype(F32).astype(jnp.int32)
        plane = tags[3:4, :]
        ku_s[:, cols] = spread(tap_rows(kern_u, plane), tags[0:1, :], 0, GU).astype(BF16)
        start = tags[1:2, :] + GV * (tags[2:3, :] - facet)
        wide = spread(tap_rows(kern_v, plane), start, 0, GV).T
        high = wide.astype(BF16)
        kv_s[cols, :GV] = high
        kv_s[cols, GV:] = (wide - high.astype(F32)).astype(BF16)

    def product(first, cols):
        vis = held_s[pl.ds(first, step_chans), cols].astype(F32)
        left = weighted(vis, ku_s[:, cols].astype(F32))
        return jnp.dot(left, kv_s[cols, :], preferred_element_type=F32)

    def copy_out(i):
        some = pl.ds(i * step_chans, step_chans)
        return pltpu.make_async_copy(grid_s.at[some], out_ref.at[some], sems.at[i])

    def emit(i, total):
        total = (total[:, :GV] + total[:, GV:]).reshape(step_chans, GU, GV)
        some = pl.ds(i * step_chans, step_chans)
        grid_s[some] = total
        strip_ref[some] = total[:, :TAPS, :]
        copy_out(i).start()

    steps = chans // step_chans
    over = sum_of_tags(half, msgs_ref)[0, 4] > 0.0

    @pl.when(over)
    def _():
        fetch = pltpu.make_async_copy(other_ref, held_s, other_sem)
        fetch.start()
        fetch.wait()
        tiles_s[0] = tiles_of(held_s)

    @pl.when(jnp.logical_not(over) & early())
    def _():
        tiles = tiles_of(held_ref)
        tiles_s[0] = tiles

        def copy_tile(k, _):
            cols = pl.ds(pl.multiple_of(k * KT, KT), KT)
            held_s[:, cols] = held_ref[:, cols]
            return 0

        lax.fori_loop(0, tiles, copy_tile, 0)

    @pl.when(jnp.logical_not(over) & jnp.logical_not(early()))
    def _():
        tiles = gather_rows(half, chans, msgs_ref, rows_s)
        tiles_s[0] = tiles
        lax.fori_loop(0, tiles, lambda k, _: (turn_tile(chans, rows_s, held_s, tiles, k), 0)[1], 0)

    tiles = tiles_s[0]
    for n in (1, 2, 3):

        @pl.when(tiles == n)
        def _(n=n):
            for k in range(n):
                prepare(k)
            for i in range(steps):
                emit(i, product(i * step_chans, pl.ds(0, n * KT)))

    @pl.when(tiles > 3)
    def _():
        lax.fori_loop(0, tiles, lambda k, _: (prepare(k), 0)[1], 0)
        for i in range(steps):
            acc[...] = jnp.zeros_like(acc)

            def step(k, _, i=i):
                acc[...] += product(i * step_chans, pl.ds(pl.multiple_of(k * KT, KT), KT))
                return 0

            lax.fori_loop(0, tiles, step, 0)
            emit(i, acc[...])

    for i in range(steps):
        copy_out(i).wait()


def main(half, msgs, held, other, tables, step_chans=16):
    depth, width = other.shape
    chans = depth - META
    vmem = pl.BlockSpec(memory_space=pltpu.VMEM)
    return pl.pallas_call(
        functools.partial(main_kernel, half, step_chans),
        out_shape=(
            jax.ShapeDtypeStruct((chans, GU, GV), F32),
            jax.ShapeDtypeStruct((chans, TAPS, GV), F32),
        ),
        in_specs=[vmem, vmem, pl.BlockSpec(memory_space=pl.ANY), vmem],
        out_specs=(pl.BlockSpec(memory_space=pl.ANY), vmem),
        scratch_shapes=[
            pltpu.VMEM(other.shape, BF16),
            pltpu.VMEM((held.shape[1] + 2 * KT, LANES), F32),
            pltpu.VMEM((chans, GU, GV), F32),
            pltpu.VMEM((GU, width), BF16),
            pltpu.VMEM((width, 2 * GV), BF16),
            pltpu.VMEM((step_chans * GU, 2 * GV), F32),
            pltpu.SemaphoreType.DMA((chans // step_chans,)),
            pltpu.SemaphoreType.DMA(()),
            pltpu.SMEM((1,), jnp.int32),
        ],
        compiler_params=pltpu.CompilerParams(vmem_limit_bytes=18 << 20),
    )(msgs, held, other, tables)


def join_kernel(_, strip_ref, halo_ref, out_ref, total, sem):
    below = jnp.where(lax.axis_index("fu") > 0, halo_ref[...].astype(F32), 0.0)
    total[...] = strip_ref[...] + below
    copy = pltpu.make_async_copy(total, out_ref.at[:, pl.ds(0, TAPS), :], sem)
    copy.start()
    copy.wait()


def join(grid, strip, halo):
    vmem = pl.BlockSpec(memory_space=pltpu.VMEM)
    whole = pl.BlockSpec(memory_space=pl.ANY)
    return pl.pallas_call(
        join_kernel,
        out_shape=jax.ShapeDtypeStruct(grid.shape, grid.dtype),
        in_specs=[whole, vmem, vmem],
        out_specs=whole,
        scratch_shapes=[pltpu.VMEM(strip.shape, F32), pltpu.SemaphoreType.DMA(())],
        input_output_aliases={0: 0},
        compiler_params=pltpu.CompilerParams(vmem_limit_bytes=2 << 20),
    )(grid, strip, halo)


def per_device(u_cell, v_cell, w_plane, counts, vis_values, kern_u, kern_v):
    n_fv = lax.axis_size("fv")
    n_fu = lax.axis_size("fu")
    rows = u_cell.shape[1]
    chans = vis_values.shape[0]
    width = 4096
    usual_half = 40
    vis = vis_values[:, 0, :]

    def exchange(half):
        sent, tables = pack(half, n_fv, u_cell, v_cell, w_plane, counts, vis, kern_u.T, kern_v.T)
        return lax.all_to_all(sent, "fv", 0, 0), tables

    msgs, tables = exchange(usual_half)
    held, halo, over, other = border(usual_half, chans, msgs, tables, width, 1)

    def whole(_):
        return border(rows // 2, chans, exchange(rows // 2)[0], tables, width, 0)

    other, halo, _ = lax.while_loop(lambda state: state[2][0, 0] > 0, whole, (other, halo, over))
    came = lax.ppermute(halo, "fu", [(i, (i + 1) % n_fu) for i in range(n_fu)])
    grid, strip = main(usual_half, msgs, held, other, tables)
    return join(grid, strip, came)


def solution(mesh):
    return jax.shard_map(
        per_device,
        mesh=mesh,
        in_specs=(
            P("fu", "fv"),
            P("fu", "fv"),
            P("fu", "fv"),
            P("fu", "fv"),
            P("ch", "fu", "fv"),
            P(),
            P(),
        ),
        out_specs=P("ch", "fu", "fv"),
        check_vma=False,
    )
```

```python
import functools

import jax
import jax.numpy as jnp
from jax import lax
from jax.experimental import pallas as pl
from jax.experimental.pallas import tpu as pltpu
from jax.sharding import PartitionSpec as P

GU = 64
GV = 128
TAPS = 8
LANES = 128
META = 8
KT = 256
F32 = jnp.float32
BF16 = jnp.bfloat16
NT = (((1,), (1,)), ((), ()))


def tag_rows(half):
    per_row = LANES // (2 * META)
    return META * (-(-half // (META * per_row)))


def pack_kernel(
    half, n_dst, u_ref, v_ref, w_ref, counts_ref, vis_ref, kern_u_ref, kern_v_ref, out_ref, tables_ref, picks_s
):
    chans, rows = vis_ref.shape
    n_blocks = counts_ref.shape[1]
    block = rows // n_blocks
    cap = 2 * half
    tables_ref[:TAPS, :] = kern_u_ref[...]
    tables_ref[TAPS:, :] = kern_v_ref[...]
    u, v, w = u_ref[...], v_ref[...], w_ref[...]
    lane = lax.broadcasted_iota(jnp.int32, (1, rows), 1)
    limit = jnp.zeros((1, rows), jnp.int32)
    for b in range(n_blocks):
        limit = jnp.where(lane >= b * block, b * block + counts_ref[0, b], limit)
    live = lane < limit
    first = v // GV
    last = (v + (TAPS - 1)) // GV
    dst = lax.broadcasted_iota(jnp.int32, (n_dst, rows), 0)
    member = ((dst == first) | (dst == last)) & live
    edge = member & (u % GU > GU - TAPS)
    plain_f = (member & jnp.logical_not(edge)).astype(F32)
    edge_f = edge.astype(F32)
    flags = jnp.concatenate([edge_f, plain_f], axis=0)
    blocks = [flags[:, at : at + LANES] for at in range(0, rows, LANES)]
    before = lax.broadcasted_iota(jnp.int32, (LANES, LANES), 0) < lax.broadcasted_iota(
        jnp.int32, (LANES, LANES), 1
    )
    inside = jnp.dot(
        jnp.concatenate(blocks, axis=0).astype(BF16),
        before.astype(F32).astype(BF16),
        preferred_element_type=F32,
    )
    seen = jnp.zeros((2 * n_dst, 1), F32)
    ranks = []
    for b, block_flags in enumerate(blocks):
        ranks.append(inside[2 * n_dst * b : 2 * n_dst * (b + 1)] + seen)
        seen = seen + jnp.sum(block_flags, axis=1, keepdims=True)
    rank = jnp.concatenate(ranks, axis=1)
    edges = seen[:n_dst]
    total = edges + seen[n_dst:]
    rank = jnp.where(edge, rank[:n_dst], rank[n_dst:] + edges)
    rank = jnp.where(member, rank.astype(jnp.int32), -1)
    over = (jnp.max(total, axis=0, keepdims=True) > cap).astype(F32)
    tags = jnp.concatenate(
        [
            (u % GU).astype(F32),
            (v % GV).astype(F32),
            first.astype(F32),
            w.astype(F32),
            jnp.zeros((META - 4, rows), F32),
        ],
        axis=0,
    )
    empty = jnp.zeros_like(tags)
    tags = jnp.concatenate(
        [
            jnp.concatenate([tags, empty], axis=1),
            jnp.concatenate([empty, tags], axis=1),
            jnp.zeros((LANES - 2 * META, 2 * rows), F32),
        ],
        axis=0,
    ).astype(BF16)
    vis = vis_ref[...]
    blank = jnp.zeros_like(vis)
    source = jnp.concatenate(
        [
            jnp.concatenate([vis, blank], axis=1),
            jnp.concatenate([blank, vis], axis=1),
            tags,
        ],
        axis=0,
    )
    slot = lax.broadcasted_iota(jnp.int32, (cap, rows), 0)
    exact = cap <= 256
    if exact:
        slot = slot.astype(F32).astype(BF16)
        rank = rank.astype(F32).astype(BF16)
    one, nought = jnp.ones((), BF16), jnp.zeros((), BF16)
    for d in range(n_dst):
        same = slot == rank[d : d + 1, :]
        pick = jnp.where(same, one, nought) if exact else same.astype(F32).astype(BF16)
        picks_s[d * half : (d + 1) * half, :rows] = pick[:half]
        picks_s[d * half : (d + 1) * half, rows:] = pick[half:]
    sent = lax.dot_general(picks_s[...], source, NT, preferred_element_type=F32)
    out_ref[:, :half, :] = sent[:, :LANES].reshape(n_dst, half, LANES).astype(BF16)
    place = lax.broadcasted_iota(jnp.int32, (META, LANES), 1)
    per_row = LANES // (2 * META)
    for d in range(n_dst):
        eights = jnp.floor((jnp.minimum(total[d : d + 1, :], float(cap)) + (META - 1)) / META)
        row = jnp.where(place == 4, over, 0.0)
        row = jnp.where(place == 5, eights, row)
        row = jnp.where(place == 6, jnp.floor((edges[d : d + 1, :] + (META - 1)) / META), row)
        for g in range(half // META):
            at = d * half + g * META
            part = sent[at : at + META, LANES:]
            shift = 2 * META * (g % per_row)
            row = row + (pltpu.roll(part, shift, 1) if shift else part)
            if g % per_row == per_row - 1 or g == half // META - 1:
                to = half + META * (g // per_row)
                out_ref[d, to : to + META, :] = row.astype(BF16)
                row = jnp.zeros((META, LANES), F32)


def pack(half, n_dst, u, v, w, counts, vis, kern_u, kern_v):
    vmem = pl.BlockSpec(memory_space=pltpu.VMEM)
    rows = u.shape[1]
    return pl.pallas_call(
        functools.partial(pack_kernel, half, n_dst),
        out_shape=(
            jax.ShapeDtypeStruct((n_dst, half + tag_rows(half), LANES), BF16),
            jax.ShapeDtypeStruct((2 * TAPS, kern_u.shape[1]), F32),
        ),
        in_specs=[vmem, vmem, vmem, pl.BlockSpec(memory_space=pltpu.SMEM), vmem, vmem, vmem],
        out_specs=(vmem, vmem),
        scratch_shapes=[pltpu.VMEM((n_dst * half, 2 * rows), BF16)],
        compiler_params=pltpu.CompilerParams(vmem_limit_bytes=(8 << 20) if half <= 64 else (24 << 20)),
    )(u, v, w, counts, vis, kern_u, kern_v)


def tap_rows(table, plane):
    result = jnp.zeros((TAPS, plane.shape[1]), F32)
    for p in range(table.shape[1]):
        result = jnp.where(plane == p, table[:, p : p + 1], result)
    return result


def spread(taps, start, low, span):
    cell = lax.broadcasted_iota(jnp.int32, (span, taps.shape[1]), 0) + (low - start)
    result = jnp.zeros((span, taps.shape[1]), F32)
    for t in range(TAPS):
        result = jnp.where(cell == t, taps[t : t + 1, :], result)
    return result


def weighted(vis, ku):
    chans, span, lanes = vis.shape[0], ku.shape[0], vis.shape[1]
    full = vis[:, None, :] * ku[None, :, :]
    return full.reshape(chans * span, lanes).astype(BF16)


def merged_rows(half, chans, msgs_ref, src, upper, groups):
    lane = lax.broadcasted_iota(jnp.int32, (META, LANES), 1)
    per_row = LANES // (2 * META)
    parts = []
    for g in groups:
        at = half + META * (g // per_row)
        vis = msgs_ref[src, g * META : (g + 1) * META, :].astype(F32)
        tag = msgs_ref[src, at : at + META, :].astype(F32)
        if upper:
            vis = pltpu.roll(vis, LANES // 2, 1)
        shift = (chans - 2 * META * (g % per_row) - META * upper) % LANES
        parts.append(jnp.where(lane < chans, vis, pltpu.roll(tag, shift, 1)))
    return jnp.concatenate(parts, axis=0)


def gather_rows(half, chans, msgs_ref, rows_s):
    n_src = msgs_ref.shape[0]
    groups = range(half // META)
    lengths = []
    for src in range(n_src):
        tags = msgs_ref[src, half : half + META, :].astype(F32)
        lengths.append(tags[0, 5].astype(jnp.int32) * META)
    offset = 0
    for src in range(n_src):
        rows_s[pl.ds(offset, half), :] = merged_rows(half, chans, msgs_ref, src, 0, groups)

        @pl.when(lengths[src] > half)
        def _(src=src, offset=offset):
            rows_s[pl.ds(offset + half, half), :] = merged_rows(half, chans, msgs_ref, src, 1, groups)

        offset = pl.multiple_of(offset + lengths[src], META)
    rows_s[pl.ds(offset, KT), :] = jnp.zeros((KT, LANES), F32)
    return jnp.maximum((offset + KT - 1) // KT, 1)


def turn_tile(chans, rows_s, held, tiles, k):
    cols = pl.ds(pl.multiple_of(k * KT, KT), KT)
    turned = rows_s[cols, :].T
    tag_id = lax.broadcasted_iota(jnp.int32, (META, KT), 0)
    tags = turned[chans : chans + META]
    held[:chans, cols] = turned[:chans].astype(BF16)
    held[chans:, cols] = jnp.where(tag_id == META - 1, tiles.astype(F32), tags).astype(BF16)


def border_product(chans, block, tables_ref):
    kern_u, kern_v = tables_ref[:TAPS, :], tables_ref[TAPS:, :]
    turned = block.T
    tags = turned[chans : chans + META].astype(jnp.int32)
    plane = tags[3:4, :]
    ku = spread(tap_rows(kern_u, plane), tags[0:1, :], GU, TAPS)
    left = weighted(turned[:chans], ku.astype(BF16).astype(F32))
    start = tags[1:2, :] + GV * (tags[2:3, :] - lax.axis_index("fv"))
    right = spread(tap_rows(kern_v, plane), start, 0, GV).astype(BF16)
    return lax.dot_general(left, right, NT, preferred_element_type=F32)


def sum_of_tags(half, msgs_ref):
    total = jnp.zeros((META, LANES), F32)
    for src in range(msgs_ref.shape[0]):
        total = total + msgs_ref[src, half : half + META, :].astype(F32)
    return total


def whole_kernel(half, chans, msgs_ref, tables_ref, held_ref, halo_ref, over_ref, rows_s, acc):
    tiles = gather_rows(half, chans, msgs_ref, rows_s)
    acc[...] = jnp.zeros_like(acc)

    def step(k, _):
        turn_tile(chans, rows_s, held_ref, tiles, k)
        block = rows_s[pl.ds(pl.multiple_of(k * KT, KT), KT), :]
        acc[...] += border_product(chans, block, tables_ref)
        return 0

    lax.fori_loop(0, tiles, step, 0)
    halo_ref[...] = acc[...].reshape(chans, TAPS, GV).astype(BF16)
    over_ref[0, 0] = 0


def early():
    return lax.axis_index("fu") % 2 == 1


def usual_kernel(half, chans, msgs_ref, tables_ref, held_ref, halo_ref, over_ref, other_ref, rows_s, acc):
    n_src = msgs_ref.shape[0]
    groups = half // META
    over_ref[0, 0] = sum_of_tags(half, msgs_ref)[0, 4].astype(jnp.int32)
    most = jnp.zeros((META, LANES), F32)
    for src in range(n_src):
        most = jnp.maximum(most, msgs_ref[src, half : half + META, :].astype(F32))
    chunks = most[0, 6].astype(jnp.int32)

    def chunk(c):
        upper, g = c // groups, c % groups
        block = [merged_rows(half, chans, msgs_ref, src, upper, [g]) for src in range(n_src)]
        return border_product(chans, jnp.concatenate(block, axis=0), tables_ref)

    def emit(total):
        halo_ref[...] = total.reshape(chans, TAPS, GV).astype(BF16)

    @pl.when(chunks <= 1)
    def _():
        emit(chunk(0))

    @pl.when(chunks > 1)
    def _():
        acc[...] = chunk(0) + chunk(1)
        for c in range(2, 2 * groups):

            @pl.when(chunks > c)
            def _(c=c):
                acc[...] += chunk(c)

        emit(acc[...])

    @pl.when(early())
    def _():
        tiles = gather_rows(half, chans, msgs_ref, rows_s)
        lax.fori_loop(0, tiles, lambda k, _: (turn_tile(chans, rows_s, held_ref, tiles, k), 0)[1], 0)


def border(half, chans, msgs, tables, width, usual):
    vmem = pl.BlockSpec(memory_space=pltpu.VMEM)
    whole = jax.ShapeDtypeStruct((chans + META, width), BF16)
    most = width
    if usual:
        most = -(-2 * half * msgs.shape[0] // KT) * KT
    return pl.pallas_call(
        functools.partial(usual_kernel if usual else whole_kernel, half, chans),
        out_shape=(
            jax.ShapeDtypeStruct((chans + META, most), BF16),
            jax.ShapeDtypeStruct((chans, TAPS, GV), BF16),
            jax.ShapeDtypeStruct((1, 1), jnp.int32),
        )
        + (whole,) * usual,
        in_specs=[vmem, vmem],
        out_specs=(vmem, vmem, pl.BlockSpec(memory_space=pltpu.SMEM))
        + (pl.BlockSpec(memory_space=pl.ANY),) * usual,
        scratch_shapes=[
            pltpu.VMEM((most + 2 * KT, LANES), F32),
            pltpu.VMEM((chans * TAPS, GV), F32),
        ],
        compiler_params=pltpu.CompilerParams(vmem_limit_bytes=12 << 20),
    )(msgs, tables)


def main_kernel(
    half, step_chans, msgs_ref, held_ref, other_ref, tables_ref, out_ref, strip_ref,
    held_s, rows_s, grid_s, ku_s, kv_s, acc, sems, other_sem, tiles_s
):
    chans = held_s.shape[0] - META
    facet = lax.axis_index("fv")
    kern_u, kern_v = tables_ref[:TAPS, :], tables_ref[TAPS:, :]

    def tiles_of(ref):
        return ref[chans:, :LANES].astype(F32)[META - 1, 0].astype(jnp.int32)

    def prepare(k):
        cols = pl.ds(pl.multiple_of(k * KT, KT), KT)
        tags = held_s[chans:, cols].astype(F32).astype(jnp.int32)
        plane = tags[3:4, :]
        ku_s[:, cols] = spread(tap_rows(kern_u, plane), tags[0:1, :], 0, GU).astype(BF16)
        start = tags[1:2, :] + GV * (tags[2:3, :] - facet)
        wide = spread(tap_rows(kern_v, plane), start, 0, GV).T
        high = wide.astype(BF16)
        kv_s[cols, :GV] = high
        kv_s[cols, GV:] = (wide - high.astype(F32)).astype(BF16)

    def product(first, cols):
        vis = held_s[pl.ds(first, step_chans), cols].astype(F32)
        left = weighted(vis, ku_s[:, cols].astype(F32))
        return jnp.dot(left, kv_s[cols, :], preferred_element_type=F32)

    def copy_out(i):
        some = pl.ds(i * step_chans, step_chans)
        return pltpu.make_async_copy(grid_s.at[some], out_ref.at[some], sems.at[i])

    def emit(i, total):
        total = (total[:, :GV] + total[:, GV:]).reshape(step_chans, GU, GV)
        some = pl.ds(i * step_chans, step_chans)
        grid_s[some] = total
        strip_ref[some] = total[:, :TAPS, :]
        copy_out(i).start()

    steps = chans // step_chans
    over = sum_of_tags(half, msgs_ref)[0, 4] > 0.0

    @pl.when(over)
    def _():
        fetch = pltpu.make_async_copy(other_ref, held_s, other_sem)
        fetch.start()
        fetch.wait()
        tiles_s[0] = tiles_of(held_s)

    @pl.when(jnp.logical_not(over) & early())
    def _():
        tiles = tiles_of(held_ref)
        tiles_s[0] = tiles

        def copy_tile(k, _):
            cols = pl.ds(pl.multiple_of(k * KT, KT), KT)
            held_s[:, cols] = held_ref[:, cols]
            return 0

        lax.fori_loop(0, tiles, copy_tile, 0)

    @pl.when(jnp.logical_not(over) & jnp.logical_not(early()))
    def _():
        tiles = gather_rows(half, chans, msgs_ref, rows_s)
        tiles_s[0] = tiles
        lax.fori_loop(0, tiles, lambda k, _: (turn_tile(chans, rows_s, held_s, tiles, k), 0)[1], 0)

    tiles = tiles_s[0]
    for n in (1, 2, 3):

        @pl.when(tiles == n)
        def _(n=n):
            for k in range(n):
                prepare(k)
            for i in range(steps):
                emit(i, product(i * step_chans, pl.ds(0, n * KT)))

    @pl.when(tiles > 3)
    def _():
        lax.fori_loop(0, tiles, lambda k, _: (prepare(k), 0)[1], 0)
        for i in range(steps):
            acc[...] = jnp.zeros_like(acc)

            def step(k, _, i=i):
                acc[...] += product(i * step_chans, pl.ds(pl.multiple_of(k * KT, KT), KT))
                return 0

            lax.fori_loop(0, tiles, step, 0)
            emit(i, acc[...])

    for i in range(steps):
        copy_out(i).wait()


def main(half, msgs, held, other, tables, step_chans=8):
    depth, width = other.shape
    chans = depth - META
    vmem = pl.BlockSpec(memory_space=pltpu.VMEM)
    return pl.pallas_call(
        functools.partial(main_kernel, half, step_chans),
        out_shape=(
            jax.ShapeDtypeStruct((chans, GU, GV), F32),
            jax.ShapeDtypeStruct((chans, TAPS, GV), F32),
        ),
        in_specs=[vmem, vmem, pl.BlockSpec(memory_space=pl.ANY), vmem],
        out_specs=(pl.BlockSpec(memory_space=pl.ANY), vmem),
        scratch_shapes=[
            pltpu.VMEM(other.shape, BF16),
            pltpu.VMEM((held.shape[1] + 2 * KT, LANES), F32),
            pltpu.VMEM((chans, GU, GV), F32),
            pltpu.VMEM((GU, width), BF16),
            pltpu.VMEM((width, 2 * GV), BF16),
            pltpu.VMEM((step_chans * GU, 2 * GV), F32),
            pltpu.SemaphoreType.DMA((chans // step_chans,)),
            pltpu.SemaphoreType.DMA(()),
            pltpu.SMEM((1,), jnp.int32),
        ],
        compiler_params=pltpu.CompilerParams(vmem_limit_bytes=18 << 20),
    )(msgs, held, other, tables)


def join_kernel(_, strip_ref, halo_ref, out_ref, total, sem):
    below = jnp.where(lax.axis_index("fu") > 0, halo_ref[...].astype(F32), 0.0)
    total[...] = strip_ref[...] + below
    copy = pltpu.make_async_copy(total, out_ref.at[:, pl.ds(0, TAPS), :], sem)
    copy.start()
    copy.wait()


def join(grid, strip, halo):
    vmem = pl.BlockSpec(memory_space=pltpu.VMEM)
    whole = pl.BlockSpec(memory_space=pl.ANY)
    return pl.pallas_call(
        join_kernel,
        out_shape=jax.ShapeDtypeStruct(grid.shape, grid.dtype),
        in_specs=[whole, vmem, vmem],
        out_specs=whole,
        scratch_shapes=[pltpu.VMEM(strip.shape, F32), pltpu.SemaphoreType.DMA(())],
        input_output_aliases={0: 0},
        compiler_params=pltpu.CompilerParams(vmem_limit_bytes=2 << 20),
    )(grid, strip, halo)


def per_device(u_cell, v_cell, w_plane, counts, vis_values, kern_u, kern_v):
    n_fv = lax.axis_size("fv")
    n_fu = lax.axis_size("fu")
    rows = u_cell.shape[1]
    chans = vis_values.shape[0]
    width = 4096
    usual_half = 40
    vis = vis_values[:, 0, :]

    def exchange(half):
        sent, tables = pack(half, n_fv, u_cell, v_cell, w_plane, counts, vis, kern_u.T, kern_v.T)
        return lax.all_to_all(sent, "fv", 0, 0), tables

    msgs, tables = exchange(usual_half)
    held, halo, over, other = border(usual_half, chans, msgs, tables, width, 1)

    def whole(_):
        return border(rows // 2, chans, exchange(rows // 2)[0], tables, width, 0)

    other, halo, _ = lax.while_loop(lambda state: state[2][0, 0] > 0, whole, (other, halo, over))
    came = lax.ppermute(halo, "fu", [(i, (i + 1) % n_fu) for i in range(n_fu)])
    grid, strip = main(usual_half, msgs, held, other, tables)
    return join(grid, strip, came)


def solution(mesh):
    return jax.shard_map(
        per_device,
        mesh=mesh,
        in_specs=(
            P("fu", "fv"),
            P("fu", "fv"),
            P("fu", "fv"),
            P("fu", "fv"),
            P("ch", "fu", "fv"),
            P(),
            P(),
        ),
        out_specs=P("ch", "fu", "fv"),
        check_vma=False,
    )
```

```python
import functools

import jax
import jax.numpy as jnp
from jax import lax
from jax.experimental import pallas as pl
from jax.experimental.pallas import tpu as pltpu
from jax.sharding import PartitionSpec as P

GU = 64
GV = 128
TAPS = 8
LANES = 128
META = 8
KT = 256
F32 = jnp.float32
BF16 = jnp.bfloat16
NT = (((1,), (1,)), ((), ()))


def tag_rows(half):
    per_row = LANES // (2 * META)
    return META * (-(-half // (META * per_row)))


def pack_kernel(
    half, n_dst, u_ref, v_ref, w_ref, counts_ref, vis_ref, kern_u_ref, kern_v_ref, out_ref, tables_ref, picks_s
):
    chans, rows = vis_ref.shape
    n_blocks = counts_ref.shape[1]
    block = rows // n_blocks
    cap = 2 * half
    tables_ref[:TAPS, :] = kern_u_ref[...]
    tables_ref[TAPS:, :] = kern_v_ref[...]
    u, v, w = u_ref[...], v_ref[...], w_ref[...]
    lane = lax.broadcasted_iota(jnp.int32, (1, rows), 1)
    limit = jnp.zeros((1, rows), jnp.int32)
    for b in range(n_blocks):
        limit = jnp.where(lane >= b * block, b * block + counts_ref[0, b], limit)
    live = lane < limit
    first = v // GV
    last = (v + (TAPS - 1)) // GV
    dst = lax.broadcasted_iota(jnp.int32, (n_dst, rows), 0)
    member = ((dst == first) | (dst == last)) & live
    edge = member & (u % GU > GU - TAPS)
    plain_f = (member & jnp.logical_not(edge)).astype(F32)
    edge_f = edge.astype(F32)
    before = lax.broadcasted_iota(jnp.int32, (rows, rows), 0) < lax.broadcasted_iota(
        jnp.int32, (rows, rows), 1
    )
    rank = jnp.dot(
        jnp.concatenate([edge_f, plain_f], axis=0).astype(BF16),
        before.astype(F32).astype(BF16),
        preferred_element_type=F32,
    )
    edges = jnp.sum(edge_f, axis=1, keepdims=True)
    total = edges + jnp.sum(plain_f, axis=1, keepdims=True)
    rank = jnp.where(edge, rank[:n_dst], rank[n_dst:] + edges)
    rank = jnp.where(member, rank.astype(jnp.int32), -1)
    over = (jnp.max(total, axis=0, keepdims=True) > cap).astype(F32)
    tags = jnp.concatenate(
        [
            (u % GU).astype(F32),
            (v % GV).astype(F32),
            first.astype(F32),
            w.astype(F32),
            jnp.zeros((META - 4, rows), F32),
        ],
        axis=0,
    )
    empty = jnp.zeros_like(tags)
    tags = jnp.concatenate(
        [
            jnp.concatenate([tags, empty], axis=1),
            jnp.concatenate([empty, tags], axis=1),
            jnp.zeros((LANES - 2 * META, 2 * rows), F32),
        ],
        axis=0,
    ).astype(BF16)
    vis = vis_ref[...]
    blank = jnp.zeros_like(vis)
    source = jnp.concatenate(
        [
            jnp.concatenate([vis, blank], axis=1),
            jnp.concatenate([blank, vis], axis=1),
            tags,
        ],
        axis=0,
    )
    slot = lax.broadcasted_iota(jnp.int32, (cap, rows), 0)
    for d in range(n_dst):
        pick = (slot == rank[d : d + 1, :]).astype(F32).astype(BF16)
        picks_s[d * half : (d + 1) * half, :rows] = pick[:half]
        picks_s[d * half : (d + 1) * half, rows:] = pick[half:]
    sent = lax.dot_general(picks_s[...], source, NT, preferred_element_type=F32)
    out_ref[:, :half, :] = sent[:, :LANES].reshape(n_dst, half, LANES).astype(BF16)
    place = lax.broadcasted_iota(jnp.int32, (META, LANES), 1)
    per_row = LANES // (2 * META)
    for d in range(n_dst):
        eights = jnp.floor((jnp.minimum(total[d : d + 1, :], float(cap)) + (META - 1)) / META)
        row = jnp.where(place == 4, over, 0.0)
        row = jnp.where(place == 5, eights, row)
        row = jnp.where(place == 6, jnp.floor((edges[d : d + 1, :] + (META - 1)) / META), row)
        for g in range(half // META):
            at = d * half + g * META
            part = sent[at : at + META, LANES:]
            shift = 2 * META * (g % per_row)
            row = row + (pltpu.roll(part, shift, 1) if shift else part)
            if g % per_row == per_row - 1 or g == half // META - 1:
                to = half + META * (g // per_row)
                out_ref[d, to : to + META, :] = row.astype(BF16)
                row = jnp.zeros((META, LANES), F32)


def pack(half, n_dst, u, v, w, counts, vis, kern_u, kern_v):
    vmem = pl.BlockSpec(memory_space=pltpu.VMEM)
    rows = u.shape[1]
    return pl.pallas_call(
        functools.partial(pack_kernel, half, n_dst),
        out_shape=(
            jax.ShapeDtypeStruct((n_dst, half + tag_rows(half), LANES), BF16),
            jax.ShapeDtypeStruct((2 * TAPS, kern_u.shape[1]), F32),
        ),
        in_specs=[vmem, vmem, vmem, pl.BlockSpec(memory_space=pltpu.SMEM), vmem, vmem, vmem],
        out_specs=(vmem, vmem),
        scratch_shapes=[pltpu.VMEM((n_dst * half, 2 * rows), BF16)],
        compiler_params=pltpu.CompilerParams(vmem_limit_bytes=(8 << 20) if half <= 64 else (24 << 20)),
    )(u, v, w, counts, vis, kern_u, kern_v)


def tap_rows(table, plane):
    result = jnp.zeros((TAPS, plane.shape[1]), F32)
    for p in range(table.shape[1]):
        result = jnp.where(plane == p, table[:, p : p + 1], result)
    return result


def spread(taps, start, low, span):
    cell = lax.broadcasted_iota(jnp.int32, (span, taps.shape[1]), 0) + (low - start)
    result = jnp.zeros((span, taps.shape[1]), F32)
    for t in range(TAPS):
        result = jnp.where(cell == t, taps[t : t + 1, :], result)
    return result


def weighted(vis, ku):
    chans, span, lanes = vis.shape[0], ku.shape[0], vis.shape[1]
    full = vis[:, None, :] * ku[None, :, :]
    return full.reshape(chans * span, lanes).astype(BF16)


def merged_rows(half, chans, msgs_ref, src, upper, groups):
    lane = lax.broadcasted_iota(jnp.int32, (META, LANES), 1)
    per_row = LANES // (2 * META)
    parts = []
    for g in groups:
        at = half + META * (g // per_row)
        vis = msgs_ref[src, g * META : (g + 1) * META, :].astype(F32)
        tag = msgs_ref[src, at : at + META, :].astype(F32)
        if upper:
            vis = pltpu.roll(vis, LANES // 2, 1)
        shift = (chans - 2 * META * (g % per_row) - META * upper) % LANES
        parts.append(jnp.where(lane < chans, vis, pltpu.roll(tag, shift, 1)))
    return jnp.concatenate(parts, axis=0)


def gather_rows(half, chans, msgs_ref, rows_s):
    n_src = msgs_ref.shape[0]
    groups = range(half // META)
    lengths = []
    for src in range(n_src):
        tags = msgs_ref[src, half : half + META, :].astype(F32)
        lengths.append(tags[0, 5].astype(jnp.int32) * META)
    offset = 0
    for src in range(n_src):
        rows_s[pl.ds(offset, half), :] = merged_rows(half, chans, msgs_ref, src, 0, groups)

        @pl.when(lengths[src] > half)
        def _(src=src, offset=offset):
            rows_s[pl.ds(offset + half, half), :] = merged_rows(half, chans, msgs_ref, src, 1, groups)

        offset = pl.multiple_of(offset + lengths[src], META)
    rows_s[pl.ds(offset, KT), :] = jnp.zeros((KT, LANES), F32)
    return jnp.maximum((offset + KT - 1) // KT, 1)


def turn_tile(chans, rows_s, held, tiles, k):
    cols = pl.ds(pl.multiple_of(k * KT, KT), KT)
    turned = rows_s[cols, :].T
    tag_id = lax.broadcasted_iota(jnp.int32, (META, KT), 0)
    tags = turned[chans : chans + META]
    held[:chans, cols] = turned[:chans].astype(BF16)
    held[chans:, cols] = jnp.where(tag_id == META - 1, tiles.astype(F32), tags).astype(BF16)


def border_product(chans, block, tables_ref):
    kern_u, kern_v = tables_ref[:TAPS, :], tables_ref[TAPS:, :]
    turned = block.T
    tags = turned[chans : chans + META].astype(jnp.int32)
    plane = tags[3:4, :]
    ku = spread(tap_rows(kern_u, plane), tags[0:1, :], GU, TAPS)
    left = weighted(turned[:chans], ku.astype(BF16).astype(F32))
    start = tags[1:2, :] + GV * (tags[2:3, :] - lax.axis_index("fv"))
    right = spread(tap_rows(kern_v, plane), start, 0, GV).astype(BF16)
    return lax.dot_general(left, right, NT, preferred_element_type=F32)


def sum_of_tags(half, msgs_ref):
    total = jnp.zeros((META, LANES), F32)
    for src in range(msgs_ref.shape[0]):
        total = total + msgs_ref[src, half : half + META, :].astype(F32)
    return total


def whole_kernel(half, chans, msgs_ref, tables_ref, held_ref, halo_ref, over_ref, rows_s, acc):
    tiles = gather_rows(half, chans, msgs_ref, rows_s)
    acc[...] = jnp.zeros_like(acc)

    def step(k, _):
        turn_tile(chans, rows_s, held_ref, tiles, k)
        block = rows_s[pl.ds(pl.multiple_of(k * KT, KT), KT), :]
        acc[...] += border_product(chans, block, tables_ref)
        return 0

    lax.fori_loop(0, tiles, step, 0)
    halo_ref[...] = acc[...].reshape(chans, TAPS, GV).astype(BF16)
    over_ref[0, 0] = 0


def early():
    return lax.axis_index("fu") % 2 == 1


def usual_kernel(half, chans, msgs_ref, tables_ref, held_ref, halo_ref, over_ref, other_ref, rows_s, acc):
    n_src = msgs_ref.shape[0]
    groups = half // META
    over_ref[0, 0] = sum_of_tags(half, msgs_ref)[0, 4].astype(jnp.int32)
    most = jnp.zeros((META, LANES), F32)
    for src in range(n_src):
        most = jnp.maximum(most, msgs_ref[src, half : half + META, :].astype(F32))
    chunks = most[0, 6].astype(jnp.int32)

    def chunk(c):
        upper, g = c // groups, c % groups
        block = [merged_rows(half, chans, msgs_ref, src, upper, [g]) for src in range(n_src)]
        return border_product(chans, jnp.concatenate(block, axis=0), tables_ref)

    def emit(total):
        halo_ref[...] = total.reshape(chans, TAPS, GV).astype(BF16)

    emit(chunk(0))

    @pl.when(chunks > 1)
    def _():
        acc[...] = chunk(0) + chunk(1)
        for c in range(2, 2 * groups):

            @pl.when(chunks > c)
            def _(c=c):
                acc[...] += chunk(c)

        emit(acc[...])

    @pl.when(early())
    def _():
        tiles = gather_rows(half, chans, msgs_ref, rows_s)
        lax.fori_loop(0, tiles, lambda k, _: (turn_tile(chans, rows_s, held_ref, tiles, k), 0)[1], 0)


def border(half, chans, msgs, tables, width, usual):
    vmem = pl.BlockSpec(memory_space=pltpu.VMEM)
    whole = jax.ShapeDtypeStruct((chans + META, width), BF16)
    most = width
    if usual:
        most = -(-2 * half * msgs.shape[0] // KT) * KT
    return pl.pallas_call(
        functools.partial(usual_kernel if usual else whole_kernel, half, chans),
        out_shape=(
            jax.ShapeDtypeStruct((chans + META, most), BF16),
            jax.ShapeDtypeStruct((chans, TAPS, GV), BF16),
            jax.ShapeDtypeStruct((1, 1), jnp.int32),
        )
        + (whole,) * usual,
        in_specs=[vmem, vmem],
        out_specs=(vmem, vmem, pl.BlockSpec(memory_space=pltpu.SMEM))
        + (pl.BlockSpec(memory_space=pl.ANY),) * usual,
        scratch_shapes=[
            pltpu.VMEM((most + 2 * KT, LANES), F32),
            pltpu.VMEM((chans * TAPS, GV), F32),
        ],
        compiler_params=pltpu.CompilerParams(vmem_limit_bytes=12 << 20),
    )(msgs, tables)


def main_kernel(
    half, step_chans, msgs_ref, held_ref, other_ref, tables_ref, out_ref, strip_ref,
    held_s, rows_s, grid_s, ku_s, kv_s, acc, sems, other_sem, tiles_s
):
    chans = held_s.shape[0] - META
    facet = lax.axis_index("fv")
    kern_u, kern_v = tables_ref[:TAPS, :], tables_ref[TAPS:, :]

    def tiles_of(ref):
        return ref[chans:, :LANES].astype(F32)[META - 1, 0].astype(jnp.int32)

    def prepare(k):
        cols = pl.ds(pl.multiple_of(k * KT, KT), KT)
        tags = held_s[chans:, cols].astype(F32).astype(jnp.int32)
        plane = tags[3:4, :]
        ku_s[:, cols] = spread(tap_rows(kern_u, plane), tags[0:1, :], 0, GU).astype(BF16)
        start = tags[1:2, :] + GV * (tags[2:3, :] - facet)
        wide = spread(tap_rows(kern_v, plane), start, 0, GV).T
        high = wide.astype(BF16)
        kv_s[cols, :GV] = high
        kv_s[cols, GV:] = (wide - high.astype(F32)).astype(BF16)

    def product(first, cols):
        vis = held_s[pl.ds(first, step_chans), cols].astype(F32)
        left = weighted(vis, ku_s[:, cols].astype(F32))
        return jnp.dot(left, kv_s[cols, :], preferred_element_type=F32)

    def copy_out(i):
        some = pl.ds(i * step_chans, step_chans)
        return pltpu.make_async_copy(grid_s.at[some], out_ref.at[some], sems.at[i])

    def emit(i, total):
        total = (total[:, :GV] + total[:, GV:]).reshape(step_chans, GU, GV)
        some = pl.ds(i * step_chans, step_chans)
        grid_s[some] = total
        strip_ref[some] = total[:, :TAPS, :]
        copy_out(i).start()

    steps = chans // step_chans
    over = sum_of_tags(half, msgs_ref)[0, 4] > 0.0

    @pl.when(over)
    def _():
        fetch = pltpu.make_async_copy(other_ref, held_s, other_sem)
        fetch.start()
        fetch.wait()
        tiles_s[0] = tiles_of(held_s)

    @pl.when(jnp.logical_not(over) & early())
    def _():
        tiles = tiles_of(held_ref)
        tiles_s[0] = tiles

        def copy_tile(k, _):
            cols = pl.ds(pl.multiple_of(k * KT, KT), KT)
            held_s[:, cols] = held_ref[:, cols]
            return 0

        lax.fori_loop(0, tiles, copy_tile, 0)

    @pl.when(jnp.logical_not(over) & jnp.logical_not(early()))
    def _():
        tiles = gather_rows(half, chans, msgs_ref, rows_s)
        tiles_s[0] = tiles
        lax.fori_loop(0, tiles, lambda k, _: (turn_tile(chans, rows_s, held_s, tiles, k), 0)[1], 0)

    tiles = tiles_s[0]
    for n in (1, 2, 3):

        @pl.when(tiles == n)
        def _(n=n):
            for k in range(n):
                prepare(k)
            for i in range(steps):
                emit(i, product(i * step_chans, pl.ds(0, n * KT)))

    @pl.when(tiles > 3)
    def _():
        lax.fori_loop(0, tiles, lambda k, _: (prepare(k), 0)[1], 0)
        for i in range(steps):
            acc[...] = jnp.zeros_like(acc)

            def step(k, _, i=i):
                acc[...] += product(i * step_chans, pl.ds(pl.multiple_of(k * KT, KT), KT))
                return 0

            lax.fori_loop(0, tiles, step, 0)
            emit(i, acc[...])

    for i in range(steps):
        copy_out(i).wait()


def main(half, msgs, held, other, tables, step_chans=16):
    depth, width = other.shape
    chans = depth - META
    vmem = pl.BlockSpec(memory_space=pltpu.VMEM)
    return pl.pallas_call(
        functools.partial(main_kernel, half, step_chans),
        out_shape=(
            jax.ShapeDtypeStruct((chans, GU, GV), F32),
            jax.ShapeDtypeStruct((chans, TAPS, GV), F32),
        ),
        in_specs=[vmem, vmem, pl.BlockSpec(memory_space=pl.ANY), vmem],
        out_specs=(pl.BlockSpec(memory_space=pl.ANY), vmem),
        scratch_shapes=[
            pltpu.VMEM(other.shape, BF16),
            pltpu.VMEM((held.shape[1] + 2 * KT, LANES), F32),
            pltpu.VMEM((chans, GU, GV), F32),
            pltpu.VMEM((GU, width), BF16),
            pltpu.VMEM((width, 2 * GV), BF16),
            pltpu.VMEM((step_chans * GU, 2 * GV), F32),
            pltpu.SemaphoreType.DMA((chans // step_chans,)),
            pltpu.SemaphoreType.DMA(()),
            pltpu.SMEM((1,), jnp.int32),
        ],
        compiler_params=pltpu.CompilerParams(vmem_limit_bytes=18 << 20),
    )(msgs, held, other, tables)


def join_kernel(_, strip_ref, halo_ref, out_ref, total, sem):
    below = jnp.where(lax.axis_index("fu") > 0, halo_ref[...].astype(F32), 0.0)
    total[...] = strip_ref[...] + below
    copy = pltpu.make_async_copy(total, out_ref.at[:, pl.ds(0, TAPS), :], sem)
    copy.start()
    copy.wait()


def join(grid, strip, halo):
    vmem = pl.BlockSpec(memory_space=pltpu.VMEM)
    whole = pl.BlockSpec(memory_space=pl.ANY)
    return pl.pallas_call(
        join_kernel,
        out_shape=jax.ShapeDtypeStruct(grid.shape, grid.dtype),
        in_specs=[whole, vmem, vmem],
        out_specs=whole,
        scratch_shapes=[pltpu.VMEM(strip.shape, F32), pltpu.SemaphoreType.DMA(())],
        input_output_aliases={0: 0},
        compiler_params=pltpu.CompilerParams(vmem_limit_bytes=2 << 20),
    )(grid, strip, halo)


def per_device(u_cell, v_cell, w_plane, counts, vis_values, kern_u, kern_v):
    n_fv = lax.axis_size("fv")
    n_fu = lax.axis_size("fu")
    rows = u_cell.shape[1]
    chans = vis_values.shape[0]
    width = 4096
    usual_half = 40
    vis = vis_values[:, 0, :]

    def exchange(half):
        sent, tables = pack(half, n_fv, u_cell, v_cell, w_plane, counts, vis, kern_u.T, kern_v.T)
        return lax.all_to_all(sent, "fv", 0, 0), tables

    msgs, tables = exchange(usual_half)
    held, halo, over, other = border(usual_half, chans, msgs, tables, width, 1)

    def whole(_):
        return border(rows // 2, chans, exchange(rows // 2)[0], tables, width, 0)

    other, halo, _ = lax.while_loop(lambda state: state[2][0, 0] > 0, whole, (other, halo, over))
    came = lax.ppermute(halo, "fu", [(i, (i + 1) % n_fu) for i in range(n_fu)])
    grid, strip = main(usual_half, msgs, held, other, tables)
    return join(grid, strip, came)


def solution(mesh):
    return jax.shard_map(
        per_device,
        mesh=mesh,
        in_specs=(
            P("fu", "fv"),
            P("fu", "fv"),
            P("fu", "fv"),
            P("fu", "fv"),
            P("ch", "fu", "fv"),
            P(),
            P(),
        ),
        out_specs=P("ch", "fu", "fv"),
        check_vma=False,
    )
```
